128 devices in a mesh: seq: 32 (over x, z, core), head: 4 (over y).
Axes of the slice: x: 4, y: 4, z: 4, core: 2. Of those that a mesh axis runs over, the one named last changes fastest.
Arguments:
- layer_input: bfloat16 [16384, 4096], P('seq', 'head'), may hold values from -6 to 6
- query_rows: bfloat16 [16384, 4096], P('seq', 'head'), may hold values from -6 to 6
- key_rows: bfloat16 [16384, 4096], P('seq', 'head'), may hold values from -6 to 6
- value_rows: bfloat16 [16384, 4096], P('seq', 'head'), may hold values from -28 to 28
- out_weight: bfloat16 [4096, 4096], P('head'), may hold values from -0.09375 to 0.09375
- norm_gain: float32 [4096], P('head'), may hold values from 0.1 to 1.9
- cotangent: bfloat16 [16384, 4096], P('seq', 'head'), may hold values from -0.09375 to 0.09375
Outputs:
- projection_gradient: float32 [4096, 3, 4096], P('seq', None, 'head')
- output_gradient: float32 [4096, 4096], P('head', 'seq')
The draws below stay inside these ranges and needn't reach their ends.
All inputs are finite; a program needn't handle non-finite values.
Results may differ from the reference program's by a relative error of at most 0.023.
Values may be sent and summed in bfloat16 or wider, within the bound.
A program may use at most 192 MiB of HBM per device.

```python
import math
import jax
import jax.numpy as jnp
from jax import lax

D = 4096
HEAD_DIM = 128
TOK_DEV = 512
HEADS = 32
LENGTH = 16384
N_SEQ = 32


def draw_value_rows(key, part):
    first, second = jax.random.split(key, 2)
    column_scale = jnp.exp(jax.random.uniform(second, (1, D), jnp.float32, 0.0, math.log(10.0)))
    base = jnp.clip(jax.random.normal(first, (LENGTH, D), jnp.float32), -6.0, 6.0)
    return (base * column_scale * 0.4).astype(jnp.bfloat16)


def strengthened(result, key, source, target, blocks, factor):
    owner, partner = [(jnp.arange(result.shape[dim]) // (result.shape[dim] // blocks)).reshape([-1 if axis == dim else 1 for axis in range(result.ndim)]) for dim in (source, target)]
    chosen = jax.random.permutation(key, blocks)[partner]
    strong = (owner == chosen) | (owner == (partner + blocks // 2) % blocks)
    return jnp.where(strong, factor * result, result)


def block_scale(own_key, dims, shards, low, largest):
    level = 1.0
    for position, parts in shards:
        steps = jax.random.uniform(jax.random.fold_in(jax.random.fold_in(own_key, 6), position), (parts,), jnp.float32, low / len(shards), largest / len(shards))
        level = level * jnp.repeat(jnp.exp(steps), dims[position] // parts).reshape((-1,) + (1,) * (len(dims) - 1 - position))
    return level


def normal_values(stream_key, dims, width, limit, cuts=(), kind=jnp.bfloat16):
    drawn = width * jax.random.normal(stream_key, dims, jnp.float32)
    if cuts:
        drawn = drawn * block_scale(stream_key, dims, cuts, -0.22, 0.18)
    return jnp.clip(drawn, -limit, limit).astype(kind)


def heavy_noise(stream_key, shape, deviation, most, cuts, heavy, kind=jnp.bfloat16):
    values = deviation * jax.random.normal(stream_key, shape, jnp.float32)
    if cuts:
        values = values * block_scale(stream_key, shape, cuts, -0.22, 0.18)
    return jnp.clip(strengthened(values, jax.random.fold_in(stream_key, 3), *heavy), -most, most).astype(kind)


def setup_inputs(seed: int = 0) -> dict:
    keys = jax.random.split(jax.random.key(seed), 8)
    layer_input = heavy_noise(keys[0], (LENGTH, D), 1.0, 6.0, ((0, 32), (1, 4)), (0, 1, 32, 2.75))
    query_rows = normal_values(keys[1], (LENGTH, D), 1.0, 6.0, ((0, 32), (1, 4)))
    key_rows = normal_values(keys[2], (LENGTH, D), 1.0, 6.0, ((0, 32), (1, 4)))
    value_rows = draw_value_rows(jax.random.fold_in(keys[7], 71), 0)
    out_weight = normal_values(keys[4], (D, D), D ** -0.5, 0.09375, ((0, 4),))
    norm_gain = jnp.clip(1.0 + 0.18 * jax.random.normal(keys[5], (D,), jnp.float32), 0.1, 1.9)
    cotangent = heavy_noise(keys[6], (LENGTH, D), (TOK_DEV * N_SEQ) ** -0.5, 0.09375, ((0, 32), (1, 4)), (0, 1, 32, 2.75))
    return {"layer_input": layer_input, "query_rows": query_rows, "key_rows": key_rows, "value_rows": value_rows, "out_weight": out_weight, "norm_gain": norm_gain, "cotangent": cotangent}


def lower_mask(count):
    rows = lax.broadcasted_iota(jnp.int32, (count, count), 0)
    cols = lax.broadcasted_iota(jnp.int32, (count, count), 1)
    return rows >= cols

def reference(layer_input, query_rows, key_rows, value_rows, out_weight, norm_gain, cotangent):
    high = lax.Precision.HIGHEST
    blocks = N_SEQ
    tokens = TOK_DEV

    def split_heads(matrix):
        return matrix.reshape(blocks, tokens, HEADS, HEAD_DIM)
    queries = split_heads(query_rows)
    key_heads = split_heads(key_rows)
    value_heads = split_heads(value_rows)
    gain = norm_gain.reshape(HEADS, HEAD_DIM)
    lower = lower_mask(tokens)[None]
    block_state = jnp.einsum('bthd,bthe->bhde', key_heads.astype(jnp.float32), value_heads.astype(jnp.float32), precision=high)
    state_in = jnp.cumsum(block_state, axis=0) - block_state
    state_low = state_in.astype(jnp.bfloat16)
    gated_grad = jnp.dot(cotangent, out_weight.T, preferred_element_type=jnp.float32)
    gated_grad = gated_grad.reshape(blocks, tokens, HEADS, HEAD_DIM)

    def forward_block(items):
        query_b, key_b, value_b, state_b, upstream = items
        q32 = query_b.astype(jnp.float32)
        k32 = key_b.astype(jnp.float32)
        v32 = value_b.astype(jnp.float32)
        scores = jnp.einsum('thd,shd->hts', q32, k32, precision=high)
        scores = jnp.where(lower, scores, 0.0).astype(jnp.bfloat16)
        attention = jnp.einsum('hts,she->the', scores.astype(jnp.float32), v32, precision=high)
        attention = attention + jnp.einsum('thd,hde->the', q32, state_b.astype(jnp.float32), precision=high)
        rms_value = jnp.sqrt(lax.optimization_barrier(jnp.mean(attention * attention, axis=-1, keepdims=True)) + 1e-05)
        normed = attention / rms_value
        gated = (normed * gain).astype(jnp.bfloat16)
        scaled = upstream * gain
        inner = lax.optimization_barrier(jnp.mean(scaled * normed, axis=-1, keepdims=True))
        pre_grad = ((scaled - normed * inner) / rms_value).astype(jnp.bfloat16)
        p32 = pre_grad.astype(jnp.float32)
        mixing = jnp.einsum('the,she->hts', p32, v32, precision=high)
        mixing = jnp.where(lower, mixing, 0.0).astype(jnp.bfloat16)
        query_grad = jnp.einsum('hts,shd->thd', mixing.astype(jnp.float32), k32, precision=high)
        query_grad = query_grad + jnp.einsum('the,hde->thd', p32, state_b.astype(jnp.float32), precision=high)
        return (gated, pre_grad, query_grad.astype(jnp.bfloat16))
    gated, pre_grad, query_grad = lax.map(forward_block, (queries, key_heads, value_heads, state_low, gated_grad))
    grad_block = jnp.einsum('bthd,bthe->bhde', queries.astype(jnp.float32), pre_grad.astype(jnp.float32), precision=high)
    grad_state = jnp.cumsum(grad_block[::-1], axis=0)[::-1] - grad_block
    grad_low = grad_state.astype(jnp.bfloat16)

    def backward_block(items):
        query_b, key_b, value_b, pre_b, grad_b = items
        q32 = query_b.astype(jnp.float32)
        k32 = key_b.astype(jnp.float32)
        v32 = value_b.astype(jnp.float32)
        p32 = pre_b.astype(jnp.float32)
        g32 = grad_b.astype(jnp.float32)
        scores = jnp.einsum('thd,shd->hts', q32, k32, precision=high)
        scores = jnp.where(lower, scores, 0.0).astype(jnp.bfloat16)
        mixing = jnp.einsum('the,she->hts', p32, v32, precision=high)
        mixing = jnp.where(lower, mixing, 0.0).astype(jnp.bfloat16)
        key_grad = jnp.einsum('hts,thd->shd', mixing.astype(jnp.float32), q32, precision=high)
        key_grad = key_grad + jnp.einsum('she,hde->shd', v32, g32, precision=high)
        value_grad = jnp.einsum('hts,the->she', scores.astype(jnp.float32), p32, precision=high)
        value_grad = value_grad + jnp.einsum('shd,hde->she', k32, g32, precision=high)
        return (key_grad.astype(jnp.bfloat16), value_grad.astype(jnp.bfloat16))
    key_grad, value_grad = lax.map(backward_block, (queries, key_heads, value_heads, pre_grad, grad_low))
    stacked = jnp.concatenate([query_grad.reshape(blocks, tokens, D), key_grad.reshape(blocks, tokens, D), value_grad.reshape(blocks, tokens, D)], axis=2)
    inputs_b = layer_input.reshape(blocks, tokens, D)
    gated_b = gated.reshape(blocks, tokens, D)
    cot_b = cotangent.reshape(blocks, tokens, D)

    def accumulate(carry, items):
        input_block, grad_rows, gated_block, cot_block = items
        term = jnp.dot(input_block.T, grad_rows, preferred_element_type=jnp.float32)
        term = lax.optimization_barrier(term.astype(jnp.bfloat16)).astype(jnp.float32)
        out_term = jnp.dot(gated_block.T, cot_block, preferred_element_type=jnp.float32)
        out_term = lax.optimization_barrier(out_term.astype(jnp.bfloat16)).astype(jnp.float32)
        return ((carry[0] + term, carry[1] + out_term), None)
    start = (jnp.zeros((D, 3 * D), jnp.float32), jnp.zeros((D, D), jnp.float32))
    totals, unused = lax.scan(accumulate, start, (inputs_b, stacked, gated_b, cot_b))
    return (totals[0].reshape(D, 3, D), totals[1])
```

```python
import jax
import jax.numpy as jnp
from jax import lax
from jax.experimental import pallas as pl
from jax.experimental.pallas import tpu as pltpu
from jax.sharding import PartitionSpec as P

HEAD_DIM = 128
F32 = jnp.float32
BF16 = jnp.bfloat16
MESH_ID = pl.DeviceIdType.MESH
COLOURS = ((True, 1), (True, -1), (False, 1), (False, -1))
RING = 4


def entering(array, axis, combine, identity, reverse):
    size, position = (lax.axis_size(axis), lax.axis_index(axis))
    everything = lax.all_gather(array.astype(jnp.bfloat16), axis)
    start = jnp.broadcast_to(jnp.asarray(identity, array.dtype), array.shape)

    def lap(k, before):
        at = size - 1 - k if reverse else k
        reached = at > position if reverse else at < position
        new = combine(before, everything[at].astype(array.dtype))
        return jnp.where(reached, new, before)

    return lax.fori_loop(0, size, lap, start)


def lower_mask(count):
    rows = lax.broadcasted_iota(jnp.int32, (count, count), 0)
    cols = lax.broadcasted_iota(jnp.int32, (count, count), 1)
    return rows >= cols


def reduce_kernel(
    left_hbm, right_hbm, proj_ref, out_ref,
    lown, lpar, rown, rpar, s1, r1, acc, s2, r2,
    load_sem, ps_sem, pr_sem, s1_send, s1_recv, s2_send, s2_recv,
):
    me = lax.axis_index("seq")
    core = lax.rem(me, 2)
    z = lax.rem(lax.div(me, 2), RING)
    x = lax.div(me, 2 * RING)
    tokens = lown.shape[-1]
    cols = s1.shape[-1]
    rows = RING * HEAD_DIM

    def at(x_, z_, core_):
        return {"seq": x_ * (2 * RING) + z_ * 2 + core_}

    def step_of(is_z, sign):
        if is_z:
            return at(x, lax.rem(z + sign + RING, RING), core)
        return at(lax.rem(x + sign + RING, RING), z, core)

    partner = at(x, z, 1 - core)

    loads = [pltpu.make_async_copy(left_hbm.at[i], lown.at[i], load_sem.at[i]) for i in range(2)]
    loads += [
        pltpu.make_async_copy(right_hbm.at[i], rown.at[i], load_sem.at[2 + i]) for i in range(4)
    ]
    for i in (0, 2, 1, 3, 4, 5):
        loads[i].start()

    barrier = pltpu.get_barrier_semaphore()
    for who in [partner] + [step_of(is_z, sign) for is_z, sign in COLOURS]:
        pl.semaphore_signal(barrier, inc=1, device_id=who, device_id_type=MESH_ID)
    pl.semaphore_wait(barrier, 5)

    swaps = [
        pltpu.make_async_remote_copy(
            lown.at[i, :, :, 1 - core], lpar.at[i], ps_sem.at[i], pr_sem.at[i],
            device_id=partner, device_id_type=MESH_ID)
        for i in range(2)
    ] + [
        pltpu.make_async_remote_copy(
            rown.at[i], rpar.at[i], ps_sem.at[2 + i], pr_sem.at[2 + i],
            device_id=partner, device_id_type=MESH_ID)
        for i in range(4)
    ]
    for i in (0, 2, 1, 3, 4, 5):
        loads[i].wait()
        swaps[i].start()
    for i in (0, 2, 1, 3, 4, 5):
        swaps[i].wait_recv()

    def term(comp, colour, d):
        side = lax.div(comp + 3, 4)
        cut = slice(colour * cols, (colour + 1) * cols)
        if COLOURS[colour][0]:
            mine, other = lown[side, :, d, core], lpar[side, :, d]
        else:
            mine, other = lown[side, d, :, core], lpar[side, d]
        value = jnp.dot(mine.reshape(rows, tokens), rown[comp, :, cut], preferred_element_type=F32)
        return value + jnp.dot(
            other.reshape(rows, tokens), rpar[comp, :, cut], preferred_element_type=F32
        )

    def first_hop(k, comp, colour):
        source = s1.at[comp, colour] if k == 0 else r1.at[k - 1, comp, colour]
        return pltpu.make_async_remote_copy(
            source, r1.at[k, comp, colour],
            s1_send.at[k, comp, colour], s1_recv.at[k, comp, colour],
            device_id=step_of(*COLOURS[colour]), device_id_type=MESH_ID)

    def second_hop(k, comp, colour):
        is_z, sign = COLOURS[colour]
        source = s2.at[comp, colour] if k == 0 else r2.at[k - 1, comp, colour]
        return pltpu.make_async_remote_copy(
            source, r2.at[k, comp, colour],
            s2_send.at[k, comp, colour], s2_recv.at[k, comp, colour],
            device_id=step_of(not is_z, sign), device_id_type=MESH_ID)

    for k in range(RING):
        @pl.loop(0, 4)
        def _(comp, k=k):
            for colour, (is_z, sign) in enumerate(COLOURS):
                place = z if is_z else x
                d = lax.rem(place - sign * (1 + k) + 2 * RING, RING)
                value = term(comp, colour, d)
                if k:
                    first_hop(k - 1, comp, colour).wait_recv()
                    value = value + r1[k - 1, comp, colour].astype(F32)
                if k == 0:
                    s1[comp, colour] = value.astype(BF16)
                elif k < RING - 1:
                    r1[k - 1, comp, colour] = value.astype(BF16)
                else:
                    acc[comp, colour] = value.reshape(RING, HEAD_DIM, cols)
                    place = x if is_z else z
                    e = lax.rem(place - sign + 2 * RING, RING)
                    s2[comp, colour] = acc[comp, colour, e].astype(BF16)
            for colour in range(4):
                if k < RING - 1:
                    first_hop(k, comp, colour).start()
                else:
                    second_hop(0, comp, colour).start()

    def second_value(k, comp, colour):
        is_z, sign = COLOURS[colour]
        place = x if is_z else z
        e = lax.rem(place - sign * (1 + k) + 2 * RING, RING)
        second_hop(k - 1, comp, colour).wait_recv()
        return acc[comp, colour, e] + r2[k - 1, comp, colour].astype(F32)

    for k in range(1, RING - 1):
        @pl.loop(0, 4)
        def _(comp, k=k):
            for colour in range(4):
                r2[k - 1, comp, colour] = second_value(k, comp, colour).astype(BF16)
            for colour in range(4):
                second_hop(k, comp, colour).start()

    for colour in range(4):
        cut = slice(colour * cols, (colour + 1) * cols)
        out_ref[cut, :] = second_value(RING - 1, 0, colour).T

    @pl.loop(1, 4)
    def _(comp):
        for colour in range(4):
            cut = slice(colour * cols, (colour + 1) * cols)
            proj_ref[comp - 1, :, cut] = second_value(RING - 1, comp, colour)

    for swap in swaps:
        swap.wait_send()

    @pl.loop(0, 4)
    def _(comp):
        for colour in range(4):
            for k in range(RING - 1):
                first_hop(k, comp, colour).wait_send()
                second_hop(k, comp, colour).wait_send()


def reduce_terms(left, right):
    tokens, width = right.shape[1:]
    cols = width // 4
    dma = pltpu.SemaphoreType.DMA
    return pl.pallas_call(
        reduce_kernel,
        out_shape=(
            jax.ShapeDtypeStruct((3, HEAD_DIM, width), F32),
            jax.ShapeDtypeStruct((width, HEAD_DIM), F32),
        ),
        in_specs=[pl.BlockSpec(memory_space=pl.ANY)] * 2,
        out_specs=(pl.BlockSpec(memory_space=pltpu.VMEM),) * 2,
        scratch_shapes=[
            pltpu.VMEM(left.shape, BF16),
            pltpu.VMEM((2, RING, RING, HEAD_DIM, tokens), BF16),
            pltpu.VMEM((4, tokens, width), BF16),
            pltpu.VMEM((4, tokens, width), BF16),
            pltpu.VMEM((4, 4, RING * HEAD_DIM, cols), BF16),
            pltpu.VMEM((RING - 1, 4, 4, RING * HEAD_DIM, cols), BF16),
            pltpu.VMEM((4, 4, RING, HEAD_DIM, cols), F32),
            pltpu.VMEM((4, 4, HEAD_DIM, cols), BF16),
            pltpu.VMEM((RING - 1, 4, 4, HEAD_DIM, cols), BF16),
            dma((6,)), dma((6,)), dma((6,)),
            dma((RING - 1, 4, 4)), dma((RING - 1, 4, 4)),
            dma((RING - 1, 4, 4)), dma((RING - 1, 4, 4)),
        ],
        compiler_params=pltpu.CompilerParams(
            collective_id=0, has_side_effects=True, vmem_limit_bytes=67043328
        ),
        name="reduce_terms",
    )(left, right)


def body(layer_input, query_rows, key_rows, value_rows, out_weight, norm_gain, cotangent):
    tokens = query_rows.shape[0]
    width = query_rows.shape[1]
    heads = width // HEAD_DIM
    input_t = lax.all_gather(layer_input.T, "head", axis=0, tiled=True)
    cot_t = lax.all_gather(cotangent.T, "head", axis=0, tiled=True)
    queries = query_rows.reshape(tokens, heads, HEAD_DIM)
    key_heads = key_rows.reshape(tokens, heads, HEAD_DIM)
    value_heads = value_rows.reshape(tokens, heads, HEAD_DIM)
    gain = norm_gain.reshape(heads, HEAD_DIM)
    lower = lower_mask(tokens)[None]
    block_state = jnp.einsum(
        "thd,the->hde", key_heads, value_heads, preferred_element_type=jnp.float32
    )
    state_in = entering(block_state, "seq", jnp.add, jnp.zeros_like(block_state), False)
    state_low = state_in.astype(jnp.bfloat16)
    scores = jnp.einsum("thd,shd->hts", queries, key_heads, preferred_element_type=jnp.float32)
    scores = jnp.where(lower, scores, 0.0).astype(jnp.bfloat16)
    attention = jnp.einsum("hts,she->the", scores, value_heads, preferred_element_type=jnp.float32)
    attention = attention + jnp.einsum(
        "thd,hde->the", queries, state_low, preferred_element_type=jnp.float32
    )
    rms_value = jnp.sqrt(jnp.mean(attention * attention, axis=-1, keepdims=True) + 1e-05)
    normed = attention / rms_value
    gated = (normed * gain).astype(jnp.bfloat16).reshape(tokens, width)
    gated_grad = jnp.einsum("jt,cj->tc", cot_t, out_weight, preferred_element_type=jnp.float32)
    scaled = gated_grad.reshape(tokens, heads, HEAD_DIM) * gain
    inner = jnp.mean(scaled * normed, axis=-1, keepdims=True)
    pre_grad = ((scaled - normed * inner) / rms_value).astype(jnp.bfloat16)
    mixing = jnp.einsum("the,she->hts", pre_grad, value_heads, preferred_element_type=jnp.float32)
    mixing = jnp.where(lower, mixing, 0.0).astype(jnp.bfloat16)
    query_grad = jnp.einsum("hts,shd->thd", mixing, key_heads, preferred_element_type=jnp.float32)
    query_grad = query_grad + jnp.einsum(
        "the,hde->thd", pre_grad, state_low, preferred_element_type=jnp.float32
    )
    query_grad = query_grad.astype(jnp.bfloat16).reshape(tokens, width)
    grad_block = jnp.einsum("thd,the->hde", queries, pre_grad, preferred_element_type=jnp.float32)
    grad_state = entering(grad_block, "seq", jnp.add, jnp.zeros_like(grad_block), True)
    grad_low = grad_state.astype(jnp.bfloat16)
    key_grad = jnp.einsum("hts,thd->shd", mixing, queries, preferred_element_type=jnp.float32)
    key_grad = key_grad + jnp.einsum(
        "she,hde->shd", value_heads, grad_low, preferred_element_type=jnp.float32
    )
    value_grad = jnp.einsum("hts,the->she", scores, pre_grad, preferred_element_type=jnp.float32)
    value_grad = value_grad + jnp.einsum(
        "shd,hde->she", key_heads, grad_low, preferred_element_type=jnp.float32
    )
    key_grad, value_grad = (
        key_grad.astype(jnp.bfloat16).reshape(tokens, width),
        value_grad.astype(jnp.bfloat16).reshape(tokens, width),
    )
    left = jnp.stack([cot_t, input_t]).reshape(2, RING, RING, 2, HEAD_DIM, tokens)
    right = jnp.stack([gated, query_grad, key_grad, value_grad])
    projection_gradient, output_gradient = reduce_terms(left, right)
    return (projection_gradient.transpose(1, 0, 2), output_gradient)


def solution(mesh):
    placed = (
        P("seq", "head"),
        P("seq", "head"),
        P("seq", "head"),
        P("seq", "head"),
        P("head", None),
        P("head"),
        P("seq", "head"),
    )
    return jax.shard_map(
        body,
        mesh=mesh,
        in_specs=placed,
        out_specs=(P("seq", None, "head"), P("head", "seq")),
        check_vma=False,
    )
```

```python
import jax
import jax.numpy as jnp
from jax import lax
from jax.experimental import pallas as pl
from jax.experimental.pallas import tpu as pltpu
from jax.sharding import PartitionSpec as P

HEAD_DIM = 128
F32 = jnp.float32
BF16 = jnp.bfloat16
MESH_ID = pl.DeviceIdType.MESH
COLOURS = ((True, 1), (True, -1), (False, 1), (False, -1))
RING = 4
ROW = 8


def dot_nn(a, b):
    return jnp.dot(a, b, preferred_element_type=F32)


def dot_nt(a, b):
    return lax.dot_general(a, b, (((1,), (1,)), ((), ())), preferred_element_type=F32)


def dot_tn(a, b):
    return jnp.dot(a.T, b, preferred_element_type=F32)


def step_kernel(
    x_hbm, q_hbm, k_hbm, v_hbm, w_hbm, gain_ref, cot_hbm,
    proj_ref, out_ref,
    lown, lpar, rown, rpar, qs, ks, vs, wbuf, att, gg, pre, s1, r1, acc, r2,
    blocks, gathered, totals, results, states,
    load_sem, g_send, g_recv, row_send, row_recv, tot_send, tot_recv, res_send, res_recv,
    lp_send, lp_recv, rp_send, rp_recv, s1_send, s1_recv, s2_send, s2_recv,
):
    me = lax.axis_index("seq")
    y = lax.axis_index("head")
    core = lax.rem(me, 2)
    z = lax.rem(lax.div(me, 2), RING)
    x = lax.div(me, ROW)
    j = lax.rem(me, ROW)
    tokens = qs.shape[0]
    width = qs.shape[1]
    half = tokens // 2
    heads = width // HEAD_DIM
    cols = s1.shape[-1]
    rows = RING * HEAD_DIM

    def at(x_, z_, core_):
        return {"seq": x_ * ROW + z_ * 2 + core_}

    def row_peer(j_):
        return {"seq": x * ROW + j_}

    def turn(a, n=RING):
        return lax.rem(a + 2 * n, n)

    def step_of(is_z, sign):
        return at(x, turn(z + sign), core) if is_z else at(turn(x + sign), z, core)

    partner = at(x, z, 1 - core)

    def remote(source, target, send, recv, who):
        return pltpu.make_async_remote_copy(
            source, target, send, recv, device_id=who, device_id_type=MESH_ID)

    def weight_load(n, chunk):
        start = pl.multiple_of(chunk * width, width)
        return pltpu.make_async_copy(
            w_hbm.at[:, pl.ds(start, width)], wbuf.at[n % 2], load_sem.at[5 + n])

    order = (y, turn(y - 1), turn(y + 1), turn(y + 2))
    load_cot = pltpu.make_async_copy(cot_hbm, rown.at[1], load_sem.at[0])
    load_k = pltpu.make_async_copy(k_hbm, ks, load_sem.at[1])
    load_v = pltpu.make_async_copy(v_hbm, vs, load_sem.at[2])
    load_x = pltpu.make_async_copy(x_hbm, rown.at[2], load_sem.at[3])
    load_q = pltpu.make_async_copy(q_hbm, qs, load_sem.at[4])
    for load in (load_cot, load_k, load_v, load_x, load_q):
        load.start()
    weight_load(0, order[0]).start()
    weight_load(1, order[1]).start()

    barrier = pltpu.get_barrier_semaphore()
    peers = [row_peer(turn(j + o, ROW)) for o in range(1, ROW)]
    peers += [at(turn(x + o), z, core) for o in range(1, RING)]
    peers += [{"head": turn(y + 1)}, {"head": turn(y - 1)}]
    for who in peers:
        pl.semaphore_signal(barrier, inc=1, device_id=who, device_id_type=MESH_ID)

    def transpose_in(side, stage):
        for i in range(heads):
            lown[side, y, i // 2, i % 2] = rown[stage, :, i * HEAD_DIM:(i + 1) * HEAD_DIM].T

    load_cot.wait()
    transpose_in(0, 1)
    pl.semaphore_wait(barrier, len(peers))

    def ring(side, sign, message, receiving=False):
        first = 0 if sign > 0 else 2
        part = first if message != 1 else 2 - first
        source = y if message < 2 else turn(y - sign)
        if receiving:
            source = turn(source - sign)
        place = lown.at[side, source, pl.ds(part, 2)]
        n = 0 if sign > 0 else 1
        return remote(
            place, place, g_send.at[side, n, message], g_recv.at[side, n, message],
            {"head": turn(y + sign)})

    def gather_own(side):
        for message in (0, 1):
            for sign in (1, -1):
                ring(side, sign, message).start()

    def gather_pass(side):
        for sign in (1, -1):
            ring(side, sign, 0, True).wait_recv()
            ring(side, sign, 2).start()

    gather_own(0)

    def row_copy(n, o, receiving=False):
        if receiving:
            place = turn(j - o, ROW)
            return remote(blocks.at[n, place], gathered.at[n, place],
                          row_send.at[n, o - 1], row_recv.at[n, o - 1], row_peer(place))
        to = turn(j + o, ROW)
        return remote(blocks.at[n, to], gathered.at[n, j],
                      row_send.at[n, o - 1], row_recv.at[n, o - 1], row_peer(to))

    def total_copy(n, o, receiving=False):
        place = turn(x - o) if receiving else x
        return remote(totals.at[n, place], totals.at[n, place],
                      tot_send.at[n, o - 1], tot_recv.at[n, o - 1], at(turn(x + o), z, core))

    def result_copy(n, o, receiving=False):
        if receiving:
            place = turn(j - o, ROW)
            return remote(results.at[n, place], states.at[n, place],
                          res_send.at[n, o - 1], res_recv.at[n, o - 1], row_peer(place))
        to = turn(j + o, ROW)
        return remote(results.at[n, to], states.at[n, j],
                      res_send.at[n, o - 1], res_recv.at[n, o - 1], row_peer(to))

    def scan_rows(n):
        gathered[n, j] = blocks[n, j]
        for o in range(1, ROW):
            row_copy(n, o).start()

    def scan_totals(n):
        for o in range(1, ROW):
            row_copy(n, o, True).wait_recv()
        total = gathered[n, 0].astype(F32)
        for i in range(1, ROW):
            total = total + gathered[n, i].astype(F32)
        totals[n, x] = total
        for o in range(1, RING):
            total_copy(n, o).start()

    def scan_results(n):
        for o in range(1, RING):
            total_copy(n, o, True).wait_recv()
        running = jnp.zeros((HEAD_DIM, HEAD_DIM), F32)
        for i in range(RING):
            counts = (i > x) if n else (i < x)
            running = running + jnp.where(counts, totals[n, i], 0.0)
        for i in (reversed(range(ROW)) if n else range(ROW)):
            results[n, i] = running.astype(BF16)
            running = running + gathered[n, i].astype(F32)
        states[n, j] = results[n, j]
        for o in range(1, ROW):
            result_copy(n, o).start()

    def scan_end(n):
        for o in range(1, ROW):
            result_copy(n, o, True).wait_recv()

    def head(ref, h):
        return ref[:, pl.ds(pl.multiple_of(h * HEAD_DIM, HEAD_DIM), HEAD_DIM)]

    def put_head(comp, h, value):
        rown[comp, :, pl.ds(pl.multiple_of(h * HEAD_DIM, HEAD_DIM), HEAD_DIM)] = value.astype(BF16)

    load_k.wait()
    load_v.wait()

    @pl.loop(0, heads)
    def _(h):
        blocks[0, h] = dot_tn(head(ks, h), head(vs, h)).astype(BF16)

    scan_rows(0)
    load_x.wait()
    transpose_in(1, 2)
    load_q.wait()
    scan_totals(0)

    lower_left = (
        lax.broadcasted_iota(jnp.int32, (tokens, half), 0)
        >= lax.broadcasted_iota(jnp.int32, (tokens, half), 1)
    )
    lower_right = lower_left[:half]

    def score_slots(h):
        return lax.div(h, 2), lax.rem(h, 2) * 2

    @pl.loop(0, heads)
    def _(h):
        q, k, v = head(qs, h), head(ks, h), head(vs, h)
        left = jnp.where(lower_left, dot_nt(q, k[:half]), 0.0).astype(BF16)
        right = jnp.where(lower_right, dot_nt(q[half:], k[half:]), 0.0).astype(BF16)
        a, b = score_slots(h)
        s1[a, b] = left
        s1[a, b + 1, :half] = right
        att[h, :half] = dot_nn(left[:half], v[:half])
        att[h, half:] = dot_nn(left[half:], v[:half]) + dot_nn(right, v[half:])

    scan_results(0)

    def grad_chunk(n):
        weight_load(n, order[n]).wait()

        @pl.loop(0, RING)
        def _(t):
            w = wbuf[n % 2, pl.ds(pl.multiple_of(t * 2 * HEAD_DIM, 2 * HEAD_DIM), 2 * HEAD_DIM), :]
            value = dot_nn(w, lown[0, order[n]].reshape(width, tokens)).T
            for i in range(2):
                piece = value[:, i * HEAD_DIM:(i + 1) * HEAD_DIM]
                if n:
                    piece = piece + gg[2 * t + i]
                gg[2 * t + i] = piece

        if n + 2 < RING:
            weight_load(n + 2, order[n + 2]).start()

    grad_chunk(0)
    gather_pass(0)
    gather_own(1)

    def normalised(h):
        a = att[h]
        inverse = lax.rsqrt(jnp.mean(a * a, axis=-1, keepdims=True) + 1e-05)
        return a * inverse, inverse

    scan_end(0)

    @pl.loop(0, heads)
    def _(h):
        att[h] = att[h] + dot_nn(head(qs, h), states[0, h])
        normed, _ = normalised(h)
        put_head(0, h, normed * gain_ref[pl.ds(h, 1), :])

    def left_swap(side, piece):
        return remote(lown.at[side, piece, :, 1 - core], lpar.at[side, piece],
                      lp_send.at[side, piece], lp_recv.at[side, piece], partner)

    def right_swap(comp):
        return remote(rown.at[comp], rpar.at[comp], rp_send.at[comp], rp_recv.at[comp], partner)

    right_swap(0).start()
    ring(0, 1, 1, True).wait_recv()
    left_swap(0, order[0]).start()
    left_swap(0, order[1]).start()
    grad_chunk(1)
    ring(0, -1, 1, True).wait_recv()
    left_swap(0, order[2]).start()
    grad_chunk(2)
    ring(0, 1, 2, True).wait_recv()
    ring(0, -1, 2, True).wait_recv()
    left_swap(0, order[3]).start()
    grad_chunk(3)

    @pl.loop(0, heads)
    def _(h):
        normed, inverse = normalised(h)
        u = gg[h] * gain_ref[pl.ds(h, 1), :]
        m = jnp.mean(u * normed, axis=-1, keepdims=True)
        p = ((u - normed * m) * inverse).astype(BF16)
        pre[h] = p
        blocks[1, h] = dot_tn(head(qs, h), p).astype(BF16)

    scan_rows(1)

    def term(comp, colour, d):
        side = lax.div(comp + 3, 4)
        cut = slice(colour * cols, (colour + 1) * cols)
        if COLOURS[colour][0]:
            mine, other = lown[side, :, d, core], lpar[side, :, d]
        else:
            mine, other = lown[side, d, :, core], lpar[side, d]
        value = dot_nn(mine.reshape(rows, tokens), rown[comp, :, cut])
        return value + dot_nn(other.reshape(rows, tokens), rpar[comp, :, cut])

    def first_hop(k, comp, colour):
        source = s1.at[comp, colour] if k == 0 else r1.at[k - 1, comp, colour]
        return remote(source, r1.at[k, comp, colour], s1_send.at[k, comp, colour],
                      s1_recv.at[k, comp, colour], step_of(*COLOURS[colour]))

    def second_hop(k, comp, colour):
        is_z, sign = COLOURS[colour]
        place = x if is_z else z
        source = acc.at[comp, colour, turn(place - sign)] if k == 0 else r2.at[k - 1, comp, colour]
        return remote(source, r2.at[k, comp, colour], s2_send.at[k, comp, colour],
                      s2_recv.at[k, comp, colour], step_of(not is_z, sign))

    def first_step(k, comp):
        for colour, (is_z, sign) in enumerate(COLOURS):
            value = term(comp, colour, turn((z if is_z else x) - sign * (1 + k)))
            if k:
                first_hop(k - 1, comp, colour).wait_recv()
                value = value + r1[k - 1, comp, colour].astype(F32)
            value = value.astype(BF16)
            if k == 0:
                s1[comp, colour] = value
            elif k < RING - 1:
                r1[k - 1, comp, colour] = value
            else:
                acc[comp, colour] = value.reshape(RING, HEAD_DIM, cols)
        for colour in range(4):
            if k < RING - 1:
                first_hop(k, comp, colour).start()
            else:
                second_hop(0, comp, colour).start()

    def second_value(k, comp, colour):
        is_z, sign = COLOURS[colour]
        e = turn((x if is_z else z) - sign * (1 + k))
        second_hop(k - 1, comp, colour).wait_recv()
        return acc[comp, colour, e].astype(F32) + r2[k - 1, comp, colour].astype(F32)

    def second_step(k, comp):
        for colour in range(4):
            r2[k - 1, comp, colour] = second_value(k, comp, colour).astype(BF16)
        for colour in range(4):
            second_hop(k, comp, colour).start()

    scan_totals(1)

    @pl.loop(0, heads)
    def _(h):
        q, k, v, p = head(qs, h), head(ks, h), head(vs, h), pre[h]
        state = states[0, h]
        left = jnp.where(lower_left, dot_nt(p, v[:half]), 0.0).astype(BF16)
        right = jnp.where(lower_right, dot_nt(p[half:], v[half:]), 0.0).astype(BF16)
        old = dot_nt(p, state)
        low = dot_nn(left, k[:half]) + old
        cut = pl.ds(pl.multiple_of(h * HEAD_DIM, HEAD_DIM), HEAD_DIM)
        rown[1, :half, cut] = low[:half].astype(BF16)
        rown[1, half:, cut] = (low[half:] + dot_nn(right, k[half:])).astype(BF16)
        att[h, :half] = dot_tn(left, q)
        att[h, half:] = dot_tn(right, q[half:])
        a, b = score_slots(h)
        gg[h, :half] = dot_tn(s1[a, b], p)
        gg[h, half:] = dot_tn(s1[a, b + 1, :half], p[half:])

    scan_results(1)
    right_swap(1).start()
    for piece in order:
        left_swap(0, piece).wait_recv()
    right_swap(0).wait_recv()
    first_step(0, 0)
    gather_pass(1)
    scan_end(1)

    @pl.loop(0, heads)
    def _(h):
        k, v = head(ks, h), head(vs, h)
        put_head(2, h, att[h] + dot_nt(v, states[1, h]))
        put_head(3, h, gg[h] + dot_nn(k, states[1, h]))

    right_swap(2).start()
    right_swap(3).start()
    first_step(1, 0)
    left_swap(1, order[0]).start()
    ring(1, 1, 1, True).wait_recv()
    left_swap(1, order[1]).start()
    ring(1, -1, 1, True).wait_recv()
    left_swap(1, order[2]).start()
    first_step(2, 0)
    ring(1, 1, 2, True).wait_recv()
    ring(1, -1, 2, True).wait_recv()
    left_swap(1, order[3]).start()
    first_step(3, 0)
    for comp in range(1, 4):
        right_swap(comp).wait_recv()
    for piece in order:
        left_swap(1, piece).wait_recv()

    for k in range(RING):
        @pl.loop(1, 4)
        def _(comp, k=k):
            first_step(k, comp)

        if 0 < k < RING - 1:
            second_step(k, 0)

    for colour in range(4):
        cut = slice(colour * cols, (colour + 1) * cols)
        out_ref[cut, :] = second_value(RING - 1, 0, colour).T

    for k in range(1, RING - 1):
        @pl.loop(1, 4)
        def _(comp, k=k):
            second_step(k, comp)

    @pl.loop(1, 4)
    def _(comp):
        for colour in range(4):
            cut = slice(colour * cols, (colour + 1) * cols)
            proj_ref[comp - 1, :, cut] = second_value(RING - 1, comp, colour)

    for side in range(2):
        for sign in (1, -1):
            for message in range(3):
                ring(side, sign, message).wait_send()
        for piece in order:
            left_swap(side, piece).wait_send()
        for o in range(1, ROW):
            row_copy(side, o).wait_send()
            result_copy(side, o).wait_send()
        for o in range(1, RING):
            total_copy(side, o).wait_send()

    @pl.loop(0, 4)
    def _(comp):
        right_swap(comp).wait_send()
        for colour in range(4):
            for k in range(RING - 1):
                first_hop(k, comp, colour).wait_send()
                second_hop(k, comp, colour).wait_send()


def body(layer_input, query_rows, key_rows, value_rows, out_weight, norm_gain, cotangent):
    tokens, width = query_rows.shape
    heads = width // HEAD_DIM
    cols = width // 4
    dma = pltpu.SemaphoreType.DMA
    square = (HEAD_DIM, HEAD_DIM)
    anywhere = pl.BlockSpec(memory_space=pl.ANY)
    inside = pl.BlockSpec(memory_space=pltpu.VMEM)
    projection_gradient, output_gradient = pl.pallas_call(
        step_kernel,
        out_shape=(
            jax.ShapeDtypeStruct((3, HEAD_DIM, width), F32),
            jax.ShapeDtypeStruct((width, HEAD_DIM), F32),
        ),
        in_specs=[anywhere] * 5 + [inside, anywhere],
        out_specs=(inside, inside),
        scratch_shapes=[
            pltpu.VMEM((2, RING, RING, 2, HEAD_DIM, tokens), BF16),
            pltpu.VMEM((2, RING, RING, HEAD_DIM, tokens), BF16),
            pltpu.VMEM((4, tokens, width), BF16),
            pltpu.VMEM((4, tokens, width), BF16),
            pltpu.VMEM((tokens, width), BF16),
            pltpu.VMEM((tokens, width), BF16),
            pltpu.VMEM((tokens, width), BF16),
            pltpu.VMEM((2, width, width), BF16),
            pltpu.VMEM((heads, tokens, HEAD_DIM), F32),
            pltpu.VMEM((heads, tokens, HEAD_DIM), F32),
            pltpu.VMEM((heads, tokens, HEAD_DIM), BF16),
            pltpu.VMEM((4, 4, RING * HEAD_DIM, cols), BF16),
            pltpu.VMEM((RING - 1, 4, 4, RING * HEAD_DIM, cols), BF16),
            pltpu.VMEM((4, 4, RING, HEAD_DIM, cols), BF16),
            pltpu.VMEM((RING - 1, 4, 4, HEAD_DIM, cols), BF16),
            pltpu.VMEM((2, ROW) + square, BF16),
            pltpu.VMEM((2, ROW) + square, BF16),
            pltpu.VMEM((2, RING) + square, F32),
            pltpu.VMEM((2, ROW) + square, BF16),
            pltpu.VMEM((2, ROW) + square, BF16),
            dma((9,)),
            dma((2, 2, 3)), dma((2, 2, 3)),
            dma((2, ROW - 1)), dma((2, ROW - 1)),
            dma((2, RING - 1)), dma((2, RING - 1)),
            dma((2, ROW - 1)), dma((2, ROW - 1)),
            dma((2, RING)), dma((2, RING)),
            dma((4,)), dma((4,)),
            dma((RING - 1, 4, 4)), dma((RING - 1, 4, 4)),
            dma((RING - 1, 4, 4)), dma((RING - 1, 4, 4)),
        ],
        compiler_params=pltpu.CompilerParams(
            collective_id=0, has_side_effects=True, vmem_limit_bytes=67043328
        ),
        name="linear_attention_backward",
    )(
        layer_input, query_rows, key_rows, value_rows, out_weight,
        norm_gain.reshape(heads, HEAD_DIM), cotangent,
    )
    return (projection_gradient.transpose(1, 0, 2), output_gradient)


def solution(mesh):
    placed = (
        P("seq", "head"),
        P("seq", "head"),
        P("seq", "head"),
        P("seq", "head"),
        P("head", None),
        P("head"),
        P("seq", "head"),
    )
    return jax.shard_map(
        body,
        mesh=mesh,
        in_specs=placed,
        out_specs=(P("seq", None, "head"), P("head", "seq")),
        check_vma=False,
    )
```

```python
import jax
import jax.numpy as jnp
from jax import lax
from jax.experimental import pallas as pl
from jax.experimental.pallas import tpu as pltpu
from jax.sharding import PartitionSpec as P

HEAD_DIM = 128
F32 = jnp.float32
BF16 = jnp.bfloat16
MESH_ID = pl.DeviceIdType.MESH
COLOURS = ((True, 1), (True, -1), (False, 1), (False, -1))
RING = 4
ROW = 8


def dot_nn(a, b):
    return jnp.dot(a, b, preferred_element_type=F32)


def dot_nt(a, b):
    return lax.dot_general(a, b, (((1,), (1,)), ((), ())), preferred_element_type=F32)


def dot_tn(a, b):
    return jnp.dot(a.T, b, preferred_element_type=F32)


def step_kernel(
    x_hbm, q_hbm, k_hbm, v_hbm, w_hbm, gain_ref, cot_hbm,
    proj_ref, out_ref,
    lown, lpar, rown, rpar, qs, ks, vs, wbuf, att, gg, pre, s1, r1, acc, r2,
    blocks, gathered, totals, results, states,
    load_sem, g_send, g_recv, row_send, row_recv, tot_send, tot_recv, res_send, res_recv,
    lp_send, lp_recv, rp_send, rp_recv, s1_send, s1_recv, s2_send, s2_recv,
):
    me = lax.axis_index("seq")
    y = lax.axis_index("head")
    core = lax.rem(me, 2)
    z = lax.rem(lax.div(me, 2), RING)
    x = lax.div(me, ROW)
    j = lax.rem(me, ROW)
    tokens = qs.shape[0]
    width = qs.shape[1]
    half = tokens // 2
    heads = width // HEAD_DIM
    cols = s1.shape[-1]
    rows = RING * HEAD_DIM

    def at(x_, z_, core_):
        return {"seq": x_ * ROW + z_ * 2 + core_}

    def row_peer(j_):
        return {"seq": x * ROW + j_}

    def turn(a, n=RING):
        return lax.rem(a + 2 * n, n)

    def step_of(is_z, sign):
        return at(x, turn(z + sign), core) if is_z else at(turn(x + sign), z, core)

    partner = at(x, z, 1 - core)

    def remote(source, target, send, recv, who):
        return pltpu.make_async_remote_copy(
            source, target, send, recv, device_id=who, device_id_type=MESH_ID)

    def weight_load(n, chunk):
        start = pl.multiple_of(chunk * width, width)
        return pltpu.make_async_copy(
            w_hbm.at[:, pl.ds(start, width)], wbuf.at[n % 2], load_sem.at[5 + n])

    order = (y, turn(y + 1), turn(y - 1), turn(y + 2))
    late = order[3]

    def arrival(source):
        away = turn(source - y)
        return away + lax.div(away, 2) * (5 - 2 * away)

    load_cot = pltpu.make_async_copy(cot_hbm, rown.at[1], load_sem.at[0])
    load_k = pltpu.make_async_copy(k_hbm, ks, load_sem.at[1])
    load_v = pltpu.make_async_copy(v_hbm, vs, load_sem.at[2])
    load_x = pltpu.make_async_copy(x_hbm, rown.at[2], load_sem.at[3])
    load_q = pltpu.make_async_copy(q_hbm, qs, load_sem.at[4])
    for load in (load_cot, load_k, load_v):
        load.start()

    barrier = pltpu.get_barrier_semaphore()
    peers = [row_peer(turn(j + o, ROW)) for o in range(1, ROW)]
    peers += [at(turn(x + o), z, core) for o in range(1, RING)]
    peers += [{"head": turn(y + 1)}, {"head": turn(y - 1)}]
    for who in peers:
        pl.semaphore_signal(barrier, inc=1, device_id=who, device_id_type=MESH_ID)

    def transpose_in(side, stage):
        for i in range(heads):
            lown[side, y, i // 2, i % 2] = rown[stage, :, i * HEAD_DIM:(i + 1) * HEAD_DIM].T

    load_cot.wait()
    load_x.start()
    load_q.start()
    weight_load(0, order[0]).start()
    weight_load(1, order[1]).start()
    transpose_in(0, 1)
    pl.semaphore_wait(barrier, len(peers))

    def ring(side, sign, message, receiving=False):
        first = 0 if sign > 0 else 2
        part = first if message != 1 else 2 - first
        source = y if message < 2 else turn(y - sign)
        if receiving:
            source = turn(source - sign)
        place = lown.at[side, source, pl.ds(part, 2)]
        n = 0 if sign > 0 else 1
        return remote(
            place, place, g_send.at[side, n, message], g_recv.at[side, n, message],
            {"head": turn(y + sign)})

    def gather_own(side):
        for message in (0, 1):
            for sign in (1, -1):
                ring(side, sign, message).start()

    def gather_pass(side):
        for sign in (1, -1):
            ring(side, sign, 0, True).wait_recv()
            ring(side, sign, 2).start()

    gather_own(0)

    def row_copy(n, o, receiving=False):
        if receiving:
            place = turn(j - o, ROW)
            return remote(blocks.at[n, place], gathered.at[n, place],
                          row_send.at[n, o - 1], row_recv.at[n, o - 1], row_peer(place))
        to = turn(j + o, ROW)
        return remote(blocks.at[n, to], gathered.at[n, j],
                      row_send.at[n, o - 1], row_recv.at[n, o - 1], row_peer(to))

    def total_copy(n, o, receiving=False):
        place = turn(x - o) if receiving else x
        return remote(totals.at[n, place], totals.at[n, place],
                      tot_send.at[n, o - 1], tot_recv.at[n, o - 1], at(turn(x + o), z, core))

    def result_copy(n, o, receiving=False):
        if receiving:
            place = turn(j - o, ROW)
            return remote(results.at[n, place], states.at[n, place],
                          res_send.at[n, o - 1], res_recv.at[n, o - 1], row_peer(place))
        to = turn(j + o, ROW)
        return remote(results.at[n, to], states.at[n, j],
                      res_send.at[n, o - 1], res_recv.at[n, o - 1], row_peer(to))

    def scan_rows(n):
        gathered[n, j] = blocks[n, j]
        for o in range(1, ROW):
            row_copy(n, o).start()

    def scan_totals(n):
        for o in range(1, ROW):
            row_copy(n, o, True).wait_recv()
        total = gathered[n, 0].astype(F32)
        for i in range(1, ROW):
            total = total + gathered[n, i].astype(F32)
        totals[n, x] = total
        for o in range(1, RING):
            total_copy(n, o).start()

    def scan_results(n):
        for o in range(1, RING):
            total_copy(n, o, True).wait_recv()
        running = jnp.zeros((HEAD_DIM, HEAD_DIM), F32)
        for i in range(RING):
            counts = (i > x) if n else (i < x)
            running = running + jnp.where(counts, totals[n, i], 0.0)
        for i in (reversed(range(ROW)) if n else range(ROW)):
            results[n, i] = running.astype(BF16)
            running = running + gathered[n, i].astype(F32)
        states[n, j] = results[n, j]
        for o in range(1, ROW):
            result_copy(n, o).start()

    def scan_end(n):
        for o in range(1, ROW):
            result_copy(n, o, True).wait_recv()

    def head(ref, h):
        return ref[:, pl.ds(pl.multiple_of(h * HEAD_DIM, HEAD_DIM), HEAD_DIM)]

    def put_head(comp, h, value):
        rown[comp, :, pl.ds(pl.multiple_of(h * HEAD_DIM, HEAD_DIM), HEAD_DIM)] = value.astype(BF16)

    def left_swap(side, n):
        return remote(lown.at[side, order[n], :, 1 - core], lpar.at[side, order[n]],
                      lp_send.at[side, n], lp_recv.at[side, n], partner)

    def right_swap(comp):
        return remote(rown.at[comp], rpar.at[comp], rp_send.at[comp], rp_recv.at[comp], partner)

    load_k.wait()
    load_v.wait()

    @pl.loop(0, heads)
    def _(h):
        blocks[0, h] = dot_tn(head(ks, h), head(vs, h)).astype(BF16)

    scan_rows(0)
    load_x.wait()
    transpose_in(1, 2)
    left_swap(0, 0).start()
    left_swap(1, 0).start()
    load_q.wait()

    lower_left = (
        lax.broadcasted_iota(jnp.int32, (tokens, half), 0)
        >= lax.broadcasted_iota(jnp.int32, (tokens, half), 1)
    )
    lower_right = lower_left[:half]

    def score_slots(h):
        return 1 + lax.div(h, 2), lax.rem(h, 2) * 2

    def score_heads(begin, end):
        @pl.loop(begin, end)
        def _(h):
            q, k, v = head(qs, h), head(ks, h), head(vs, h)
            left = jnp.where(lower_left, dot_nt(q, k[:half]), 0.0).astype(BF16)
            right = jnp.where(lower_right, dot_nt(q[half:], k[half:]), 0.0).astype(BF16)
            a, b = score_slots(h)
            s1[a, b] = left
            s1[a, b + 1, :half] = right
            att[h, :half] = dot_nn(left[:half], v[:half])
            att[h, half:] = dot_nn(left[half:], v[:half]) + dot_nn(right, v[half:])

    score_heads(0, heads // 2)
    scan_totals(0)
    score_heads(heads // 2, heads)
    scan_results(0)

    def grad_chunk(n):
        weight_load(n, order[n]).wait()

        @pl.loop(0, RING)
        def _(t):
            w = wbuf[n % 2, pl.ds(pl.multiple_of(t * 2 * HEAD_DIM, 2 * HEAD_DIM), 2 * HEAD_DIM), :]
            value = dot_nn(w, lown[0, order[n]].reshape(width, tokens)).T
            for i in range(2):
                piece = value[:, i * HEAD_DIM:(i + 1) * HEAD_DIM]
                if n:
                    piece = piece + gg[2 * t + i]
                gg[2 * t + i] = piece

        if n + 2 < RING:
            weight_load(n + 2, order[n + 2]).start()

    gather_pass(0)
    gather_own(1)
    grad_chunk(0)

    def normalised(h):
        a = att[h]
        inverse = lax.rsqrt(jnp.mean(a * a, axis=-1, keepdims=True) + 1e-05)
        return a * inverse, inverse

    scan_end(0)

    @pl.loop(0, heads)
    def _(h):
        att[h] = att[h] + dot_nn(head(qs, h), states[0, h])
        normed, _ = normalised(h)
        put_head(0, h, normed * gain_ref[pl.ds(h, 1), :])

    right_swap(0).start()

    def term(comp, colour, d, groups=range(RING)):
        side = lax.div(comp + 3, 4)
        cut = slice(colour * cols, (colour + 1) * cols)
        if COLOURS[colour][0]:
            mine = jnp.concatenate([lown[side, order[n], d, core] for n in groups], axis=0)
            other = jnp.concatenate([lpar[side, order[n], d] for n in groups], axis=0)
        else:
            mine = lown[side, d, :, core].reshape(rows, tokens)
            other = lpar[side, d].reshape(rows, tokens)
        return dot_nn(mine, rown[comp, :, cut]) + dot_nn(other, rpar[comp, :, cut])

    def first_hop(k, comp, colour, part=0):
        source = s1.at[comp, colour] if k == 0 else r1.at[k - 1, comp, colour]
        target = r1.at[k, comp, colour]
        if k == 0 and COLOURS[colour][0]:
            piece = pl.ds(3 * HEAD_DIM, HEAD_DIM) if part else pl.ds(0, 3 * HEAD_DIM)
            source, target = source.at[piece], target.at[piece]
        return remote(source, target, s1_send.at[k + 3 * part, comp, colour],
                      s1_recv.at[k + 3 * part, comp, colour], step_of(*COLOURS[colour]))

    def second_place(colour, k):
        is_z, sign = COLOURS[colour]
        e = turn((x if is_z else z) - sign * (1 + k))
        return arrival(e) if is_z else e

    def second_hop(k, comp, colour):
        is_z, sign = COLOURS[colour]
        source = acc.at[comp, colour, second_place(colour, 0)] if k == 0 else r2.at[k - 1, comp, colour]
        return remote(source, r2.at[k, comp, colour], s2_send.at[k, comp, colour],
                      s2_recv.at[k, comp, colour], step_of(not is_z, sign))

    def zero_step(comp, part):
        for colour in (0, 1):
            d = turn(z - COLOURS[colour][1])
            groups = range(3, 4) if part else range(3)
            piece = slice(3 * HEAD_DIM, rows) if part else slice(0, 3 * HEAD_DIM)
            s1[comp, colour, piece] = term(comp, colour, d, groups).astype(BF16)
        for colour in (0, 1):
            first_hop(0, comp, colour, part).start()
        for colour in (2, 3):
            d = turn(x - COLOURS[colour][1])

            @pl.when((d == late) if part else (d != late))
            def _(colour=colour, d=d):
                s1[comp, colour] = term(comp, colour, d).astype(BF16)
                first_hop(0, comp, colour).start()

    def first_step(k, comp):
        for colour, (is_z, sign) in enumerate(COLOURS):
            value = term(comp, colour, turn((z if is_z else x) - sign * (1 + k)))
            first_hop(k - 1, comp, colour).wait_recv()
            if k == 1 and is_z:
                first_hop(0, comp, colour, 1).wait_recv()
            value = (value + r1[k - 1, comp, colour].astype(F32)).astype(BF16)
            if k < RING - 1:
                r1[k - 1, comp, colour] = value
            else:
                acc[comp, colour] = value.reshape(RING, HEAD_DIM, cols)
        for colour in range(4):
            if k < RING - 1:
                first_hop(k, comp, colour).start()
            else:
                second_hop(0, comp, colour).start()

    def second_value(k, comp, colour):
        second_hop(k - 1, comp, colour).wait_recv()
        return (acc[comp, colour, second_place(colour, k)].astype(F32)
                + r2[k - 1, comp, colour].astype(F32))

    def second_step(k, comp):
        for colour in range(4):
            r2[k - 1, comp, colour] = second_value(k, comp, colour).astype(BF16)
        for colour in range(4):
            second_hop(k, comp, colour).start()

    ring(0, -1, 1, True).wait_recv()
    left_swap(0, 1).start()
    grad_chunk(1)
    ring(0, 1, 1, True).wait_recv()
    left_swap(0, 2).start()
    grad_chunk(2)
    for n in range(3):
        left_swap(0, n).wait_recv()
    right_swap(0).wait_recv()
    zero_step(0, 0)
    ring(0, 1, 2, True).wait_recv()
    ring(0, -1, 2, True).wait_recv()
    left_swap(0, 3).start()
    grad_chunk(3)
    left_swap(0, 3).wait_recv()
    zero_step(0, 1)

    @pl.loop(0, heads)
    def _(h):
        normed, inverse = normalised(h)
        u = gg[h] * gain_ref[pl.ds(h, 1), :]
        m = jnp.mean(u * normed, axis=-1, keepdims=True)
        p = ((u - normed * m) * inverse).astype(BF16)
        pre[h] = p
        blocks[1, h] = dot_tn(head(qs, h), p).astype(BF16)

    scan_rows(1)

    def mixing_heads(begin, end):
        @pl.loop(begin, end)
        def _(h):
            q, k, v, p = head(qs, h), head(ks, h), head(vs, h), pre[h]
            state = states[0, h]
            left = jnp.where(lower_left, dot_nt(p, v[:half]), 0.0).astype(BF16)
            right = jnp.where(lower_right, dot_nt(p[half:], v[half:]), 0.0).astype(BF16)
            low = dot_nn(left, k[:half]) + dot_nt(p, state)
            cut = pl.ds(pl.multiple_of(h * HEAD_DIM, HEAD_DIM), HEAD_DIM)
            rown[1, :half, cut] = low[:half].astype(BF16)
            rown[1, half:, cut] = (low[half:] + dot_nn(right, k[half:])).astype(BF16)
            att[h, :half] = dot_tn(left, q)
            att[h, half:] = dot_tn(right, q[half:])
            a, b = score_slots(h)
            gg[h, :half] = dot_tn(s1[a, b], p)
            gg[h, half:] = dot_tn(s1[a, b + 1, :half], p[half:])

    mixing_heads(0, heads // 2)
    scan_totals(1)
    first_step(1, 0)
    mixing_heads(heads // 2, heads)
    right_swap(1).start()
    scan_results(1)
    gather_pass(1)
    first_step(2, 0)
    scan_end(1)

    @pl.loop(0, heads)
    def _(h):
        k, v = head(ks, h), head(vs, h)
        put_head(2, h, att[h] + dot_nt(v, states[1, h]))
        put_head(3, h, gg[h] + dot_nn(k, states[1, h]))

    right_swap(2).start()
    right_swap(3).start()
    ring(1, -1, 1, True).wait_recv()
    left_swap(1, 1).start()
    ring(1, 1, 1, True).wait_recv()
    left_swap(1, 2).start()
    first_step(3, 0)
    for n in range(3):
        left_swap(1, n).wait_recv()

    @pl.loop(1, 4)
    def _(comp):
        right_swap(comp).wait_recv()
        zero_step(comp, 0)

    second_step(1, 0)
    ring(1, 1, 2, True).wait_recv()
    ring(1, -1, 2, True).wait_recv()
    left_swap(1, 3).start()
    second_step(2, 0)
    left_swap(1, 3).wait_recv()

    @pl.loop(1, 4)
    def _(comp):
        zero_step(comp, 1)

    for colour in range(4):
        cut = slice(colour * cols, (colour + 1) * cols)
        out_ref[cut, :] = second_value(RING - 1, 0, colour).T

    for k in range(1, RING):
        @pl.loop(1, 4)
        def _(comp, k=k):
            first_step(k, comp)

    for k in range(1, RING - 1):
        @pl.loop(1, 4)
        def _(comp, k=k):
            second_step(k, comp)

    @pl.loop(1, 4)
    def _(comp):
        for colour in range(4):
            cut = slice(colour * cols, (colour + 1) * cols)
            proj_ref[comp - 1, :, cut] = second_value(RING - 1, comp, colour)

    for side in range(2):
        for sign in (1, -1):
            for message in range(3):
                ring(side, sign, message).wait_send()
        for n in range(RING):
            left_swap(side, n).wait_send()
        for o in range(1, ROW):
            row_copy(side, o).wait_send()
            result_copy(side, o).wait_send()
        for o in range(1, RING):
            total_copy(side, o).wait_send()

    @pl.loop(0, 4)
    def _(comp):
        right_swap(comp).wait_send()
        for colour in range(4):
            for k in range(RING - 1):
                first_hop(k, comp, colour).wait_send()
                second_hop(k, comp, colour).wait_send()
            if COLOURS[colour][0]:
                first_hop(0, comp, colour, 1).wait_send()


def body(layer_input, query_rows, key_rows, value_rows, out_weight, norm_gain, cotangent):
    tokens, width = query_rows.shape
    heads = width // HEAD_DIM
    cols = width // 4
    dma = pltpu.SemaphoreType.DMA
    square = (HEAD_DIM, HEAD_DIM)
    anywhere = pl.BlockSpec(memory_space=pl.ANY)
    inside = pl.BlockSpec(memory_space=pltpu.VMEM)
    projection_gradient, output_gradient = pl.pallas_call(
        step_kernel,
        out_shape=(
            jax.ShapeDtypeStruct((3, HEAD_DIM, width), F32),
            jax.ShapeDtypeStruct((width, HEAD_DIM), F32),
        ),
        in_specs=[anywhere] * 5 + [inside, anywhere],
        out_specs=(inside, inside),
        scratch_shapes=[
            pltpu.VMEM((2, RING, RING, 2, HEAD_DIM, tokens), BF16),
            pltpu.VMEM((2, RING, RING, HEAD_DIM, tokens), BF16),
            pltpu.VMEM((4, tokens, width), BF16),
            pltpu.VMEM((4, tokens, width), BF16),
            pltpu.VMEM((tokens, width), BF16),
            pltpu.VMEM((tokens, width), BF16),
            pltpu.VMEM((tokens, width), BF16),
            pltpu.VMEM((2, width, width), BF16),
            pltpu.VMEM((heads, tokens, HEAD_DIM), F32),
            pltpu.VMEM((heads, tokens, HEAD_DIM), F32),
            pltpu.VMEM((heads, tokens, HEAD_DIM), BF16),
            pltpu.VMEM((5, 4, RING * HEAD_DIM, cols), BF16),
            pltpu.VMEM((RING - 1, 4, 4, RING * HEAD_DIM, cols), BF16),
            pltpu.VMEM((4, 4, RING, HEAD_DIM, cols), BF16),
            pltpu.VMEM((RING - 1, 4, 4, HEAD_DIM, cols), BF16),
            pltpu.VMEM((2, ROW) + square, BF16),
            pltpu.VMEM((2, ROW) + square, BF16),
            pltpu.VMEM((2, RING) + square, F32),
            pltpu.VMEM((2, ROW) + square, BF16),
            pltpu.VMEM((2, ROW) + square, BF16),
            dma((9,)),
            dma((2, 2, 3)), dma((2, 2, 3)),
            dma((2, ROW - 1)), dma((2, ROW - 1)),
            dma((2, RING - 1)), dma((2, RING - 1)),
            dma((2, ROW - 1)), dma((2, ROW - 1)),
            dma((2, RING)), dma((2, RING)),
            dma((4,)), dma((4,)),
            dma((RING, 4, 4)), dma((RING, 4, 4)),
            dma((RING - 1, 4, 4)), dma((RING - 1, 4, 4)),
        ],
        compiler_params=pltpu.CompilerParams(
            collective_id=0, has_side_effects=True, vmem_limit_bytes=67043328
        ),
        name="linear_attention_backward",
    )(
        layer_input, query_rows, key_rows, value_rows, out_weight,
        norm_gain.reshape(heads, HEAD_DIM), cotangent,
    )
    return (projection_gradient.transpose(1, 0, 2), output_gradient)


def solution(mesh):
    placed = (
        P("seq", "head"),
        P("seq", "head"),
        P("seq", "head"),
        P("seq", "head"),
        P("head", None),
        P("head"),
        P("seq", "head"),
    )
    return jax.shard_map(
        body,
        mesh=mesh,
        in_specs=placed,
        out_specs=(P("seq", None, "head"), P("head", "seq")),
        check_vma=False,
    )
```

```python
import jax
import jax.numpy as jnp
from jax import lax
from jax.experimental import pallas as pl
from jax.experimental.pallas import tpu as pltpu
from jax.sharding import PartitionSpec as P

HEAD_DIM = 128
F32 = jnp.float32
BF16 = jnp.bfloat16
MESH_ID = pl.DeviceIdType.MESH
COLOURS = ((True, 1), (True, -1), (False, 1), (False, -1))
RING = 4
ROW = 8


def dot_nn(a, b):
    return jnp.dot(a, b, preferred_element_type=F32)


def dot_nt(a, b):
    return lax.dot_general(a, b, (((1,), (1,)), ((), ())), preferred_element_type=F32)


def dot_tn(a, b):
    return jnp.dot(a.T, b, preferred_element_type=F32)


def step_kernel(
    x_hbm, q_hbm, k_hbm, v_hbm, w_hbm, gain_ref, cot_hbm,
    proj_ref, out_ref,
    lown, lpar, rown, rpar, qs, ks, vs, wbuf, att, gg, pre, s1, r1, acc, r2,
    blocks, gathered, totals, results, states,
    load_sem, g_send, g_recv, row_send, row_recv, tot_send, tot_recv, res_send, res_recv,
    lp_send, lp_recv, rp_send, rp_recv, s1_send, s1_recv, s2_send, s2_recv,
):
    me = lax.axis_index("seq")
    y = lax.axis_index("head")
    core = lax.rem(me, 2)
    z = lax.rem(lax.div(me, 2), RING)
    x = lax.div(me, ROW)
    j = lax.rem(me, ROW)
    tokens = qs.shape[0]
    width = qs.shape[1]
    half = tokens // 2
    heads = width // HEAD_DIM
    cols = s1.shape[-1]
    rows = RING * HEAD_DIM

    def at(x_, z_, core_):
        return {"seq": x_ * ROW + z_ * 2 + core_}

    def row_peer(j_):
        return {"seq": x * ROW + j_}

    def turn(a, n=RING):
        return lax.rem(a + 2 * n, n)

    def step_of(is_z, sign):
        return at(x, turn(z + sign), core) if is_z else at(turn(x + sign), z, core)

    partner = at(x, z, 1 - core)

    def remote(source, target, send, recv, who):
        return pltpu.make_async_remote_copy(
            source, target, send, recv, device_id=who, device_id_type=MESH_ID)

    def weight_load(n, chunk):
        start = pl.multiple_of(chunk * width, width)
        return pltpu.make_async_copy(
            w_hbm.at[:, pl.ds(start, width)], wbuf.at[n % 2], load_sem.at[5 + n])

    order = (y, turn(y + 1), turn(y - 1), turn(y + 2))
    late = order[3]

    def arrival(source):
        away = turn(source - y)
        return away + lax.div(away, 2) * (5 - 2 * away)

    load_cot = pltpu.make_async_copy(cot_hbm, rown.at[1], load_sem.at[0])
    load_k = pltpu.make_async_copy(k_hbm, ks, load_sem.at[1])
    load_v = pltpu.make_async_copy(v_hbm, vs, load_sem.at[2])
    load_x = pltpu.make_async_copy(x_hbm, rown.at[2], load_sem.at[3])
    load_q = pltpu.make_async_copy(q_hbm, qs, load_sem.at[4])
    for load in (load_cot, load_k, load_v):
        load.start()

    barrier = pltpu.get_barrier_semaphore()
    peers = [row_peer(turn(j + o, ROW)) for o in range(1, ROW)]
    peers += [at(turn(x + o), z, core) for o in range(1, RING)]
    peers += [{"head": turn(y + 1)}, {"head": turn(y - 1)}]
    for who in peers:
        pl.semaphore_signal(barrier, inc=1, device_id=who, device_id_type=MESH_ID)

    def transpose_in(side, stage):
        for i in range(heads):
            lown[side, y, i // 2, i % 2] = rown[stage, :, i * HEAD_DIM:(i + 1) * HEAD_DIM].T

    load_cot.wait()
    load_x.start()
    load_q.start()
    weight_load(0, order[0]).start()
    weight_load(1, order[1]).start()
    transpose_in(0, 1)
    pl.semaphore_wait(barrier, len(peers))

    def ring(side, sign, message, receiving=False):
        first = 0 if sign > 0 else 2
        part = first if message != 1 else 2 - first
        source = y if message < 2 else turn(y - sign)
        if receiving:
            source = turn(source - sign)
        place = lown.at[side, source, pl.ds(part, 2)]
        n = 0 if sign > 0 else 1
        return remote(
            place, place, g_send.at[side, n, message], g_recv.at[side, n, message],
            {"head": turn(y + sign)})

    def gather_own(side):
        for message in (0, 1):
            for sign in (1, -1):
                ring(side, sign, message).start()

    def gather_pass(side):
        for sign in (1, -1):
            ring(side, sign, 0, True).wait_recv()
            ring(side, sign, 2).start()

    gather_own(0)

    def row_copy(n, o, receiving=False):
        if receiving:
            place = turn(j - o, ROW)
            return remote(blocks.at[n, place], gathered.at[n, place],
                          row_send.at[n, o - 1], row_recv.at[n, o - 1], row_peer(place))
        to = turn(j + o, ROW)
        return remote(blocks.at[n, to], gathered.at[n, j],
                      row_send.at[n, o - 1], row_recv.at[n, o - 1], row_peer(to))

    def total_copy(n, o, receiving=False):
        place = turn(x - o) if receiving else x
        return remote(totals.at[n, place], totals.at[n, place],
                      tot_send.at[n, o - 1], tot_recv.at[n, o - 1], at(turn(x + o), z, core))

    def result_copy(n, o, receiving=False):
        if receiving:
            place = turn(j - o, ROW)
            return remote(results.at[n, place], states.at[n, place],
                          res_send.at[n, o - 1], res_recv.at[n, o - 1], row_peer(place))
        to = turn(j + o, ROW)
        return remote(results.at[n, to], states.at[n, j],
                      res_send.at[n, o - 1], res_recv.at[n, o - 1], row_peer(to))

    def scan_rows(n):
        gathered[n, j] = blocks[n, j]
        for o in range(1, ROW):
            row_copy(n, o).start()

    def scan_totals(n):
        for o in range(1, ROW):
            row_copy(n, o, True).wait_recv()
        total = gathered[n, 0].astype(F32)
        for i in range(1, ROW):
            total = total + gathered[n, i].astype(F32)
        totals[n, x] = total
        for o in range(1, RING):
            total_copy(n, o).start()

    def scan_results(n):
        for o in range(1, RING):
            total_copy(n, o, True).wait_recv()
        running = jnp.zeros((HEAD_DIM, HEAD_DIM), F32)
        for i in range(RING):
            counts = (i > x) if n else (i < x)
            running = running + jnp.where(counts, totals[n, i], 0.0)
        for i in (reversed(range(ROW)) if n else range(ROW)):
            results[n, i] = running.astype(BF16)
            running = running + gathered[n, i].astype(F32)
        states[n, j] = results[n, j]
        for o in range(1, ROW):
            result_copy(n, o).start()

    def scan_end(n):
        for o in range(1, ROW):
            result_copy(n, o, True).wait_recv()

    def head(ref, h):
        return ref[:, pl.ds(pl.multiple_of(h * HEAD_DIM, HEAD_DIM), HEAD_DIM)]

    def put_head(comp, h, value):
        rown[comp, :, pl.ds(pl.multiple_of(h * HEAD_DIM, HEAD_DIM), HEAD_DIM)] = value.astype(BF16)

    def left_swap(side, n):
        return remote(lown.at[side, order[n], :, 1 - core], lpar.at[side, order[n]],
                      lp_send.at[side, n], lp_recv.at[side, n], partner)

    def right_swap(comp):
        return remote(rown.at[comp], rpar.at[comp], rp_send.at[comp], rp_recv.at[comp], partner)

    load_k.wait()
    load_v.wait()

    @pl.loop(0, heads)
    def _(h):
        blocks[0, h] = dot_tn(head(ks, h), head(vs, h)).astype(BF16)

    scan_rows(0)
    load_x.wait()
    transpose_in(1, 2)
    left_swap(0, 0).start()
    left_swap(1, 0).start()
    load_q.wait()

    lower_left = (
        lax.broadcasted_iota(jnp.int32, (tokens, half), 0)
        >= lax.broadcasted_iota(jnp.int32, (tokens, half), 1)
    )
    lower_right = lower_left[:half]

    def score_slots(h):
        return 1 + lax.div(h, 2), lax.rem(h, 2) * 2

    def score_heads(begin, end):
        @pl.loop(begin, end)
        def _(h):
            q, k, v = head(qs, h), head(ks, h), head(vs, h)
            left = jnp.where(lower_left, dot_nt(q, k[:half]), 0.0).astype(BF16)
            right = jnp.where(lower_right, dot_nt(q[half:], k[half:]), 0.0).astype(BF16)
            a, b = score_slots(h)
            s1[a, b] = left
            s1[a, b + 1, :half] = right
            att[h, :half] = dot_nn(left[:half], v[:half])
            att[h, half:] = dot_nn(left[half:], v[:half]) + dot_nn(right, v[half:])

    score_heads(0, heads // 2)
    scan_totals(0)
    score_heads(heads // 2, heads)
    scan_results(0)

    def grad_chunk(n):
        weight_load(n, order[n]).wait()

        @pl.loop(0, RING)
        def _(t):
            w = wbuf[n % 2, pl.ds(pl.multiple_of(t * 2 * HEAD_DIM, 2 * HEAD_DIM), 2 * HEAD_DIM), :]
            value = dot_nn(w, lown[0, order[n]].reshape(width, tokens)).T
            for i in range(2):
                piece = value[:, i * HEAD_DIM:(i + 1) * HEAD_DIM]
                if n:
                    piece = piece + gg[2 * t + i]
                gg[2 * t + i] = piece

        if n + 2 < RING:
            weight_load(n + 2, order[n + 2]).start()

    gather_pass(0)
    gather_own(1)
    grad_chunk(0)

    def normalised(h):
        a = att[h]
        inverse = lax.rsqrt(jnp.mean(a * a, axis=-1, keepdims=True) + 1e-05)
        return a * inverse, inverse

    scan_end(0)

    @pl.loop(0, heads)
    def _(h):
        att[h] = att[h] + dot_nn(head(qs, h), states[0, h])
        normed, _ = normalised(h)
        put_head(0, h, normed * gain_ref[pl.ds(h, 1), :])

    right_swap(0).start()

    def term(comp, colour, d, groups=range(RING)):
        side = lax.div(comp + 3, 4)
        cut = slice(colour * cols, (colour + 1) * cols)
        if COLOURS[colour][0]:
            mine = jnp.concatenate([lown[side, order[n], d, core] for n in groups], axis=0)
            other = jnp.concatenate([lpar[side, order[n], d] for n in groups], axis=0)
        else:
            mine = lown[side, d, :, core].reshape(rows, tokens)
            other = lpar[side, d].reshape(rows, tokens)
        return dot_nn(mine, rown[comp, :, cut]) + dot_nn(other, rpar[comp, :, cut])

    def first_hop(k, comp, colour, part=0):
        source = s1.at[comp, colour] if k == 0 else r1.at[k - 1, comp, colour]
        target = r1.at[k, comp, colour]
        if k == 0 and COLOURS[colour][0]:
            piece = pl.ds(3 * HEAD_DIM, HEAD_DIM) if part else pl.ds(0, 3 * HEAD_DIM)
            source, target = source.at[piece], target.at[piece]
        return remote(source, target, s1_send.at[k + 3 * part, comp, colour],
                      s1_recv.at[k + 3 * part, comp, colour], step_of(*COLOURS[colour]))

    def second_place(colour, k):
        is_z, sign = COLOURS[colour]
        e = turn((x if is_z else z) - sign * (1 + k))
        return arrival(e) if is_z else e

    def second_hop(k, comp, colour):
        is_z, sign = COLOURS[colour]
        source = acc.at[comp, colour, second_place(colour, 0)] if k == 0 else r2.at[k - 1, comp, colour]
        return remote(source, r2.at[k, comp, colour], s2_send.at[k, comp, colour],
                      s2_recv.at[k, comp, colour], step_of(not is_z, sign))

    def zero_step(comp, part):
        for colour in (0, 1):
            d = turn(z - COLOURS[colour][1])
            groups = range(3, 4) if part else range(3)
            piece = slice(3 * HEAD_DIM, rows) if part else slice(0, 3 * HEAD_DIM)
            s1[comp, colour, piece] = term(comp, colour, d, groups).astype(BF16)
        for colour in (0, 1):
            first_hop(0, comp, colour, part).start()
        for colour in (2, 3):
            d = turn(x - COLOURS[colour][1])

            @pl.when((d == late) if part else (d != late))
            def _(colour=colour, d=d):
                s1[comp, colour] = term(comp, colour, d).astype(BF16)
                first_hop(0, comp, colour).start()

    def first_step(k, comp):
        for colour, (is_z, sign) in enumerate(COLOURS):
            value = term(comp, colour, turn((z if is_z else x) - sign * (1 + k)))
            first_hop(k - 1, comp, colour).wait_recv()
            if k == 1 and is_z:
                first_hop(0, comp, colour, 1).wait_recv()
            value = (value + r1[k - 1, comp, colour].astype(F32)).astype(BF16)
            if k < RING - 1:
                r1[k - 1, comp, colour] = value
            else:
                acc[comp, colour] = value.reshape(RING, HEAD_DIM, cols)
        for colour in range(4):
            if k < RING - 1:
                first_hop(k, comp, colour).start()
            else:
                second_hop(0, comp, colour).start()

    def second_value(k, comp, colour):
        second_hop(k - 1, comp, colour).wait_recv()
        return (acc[comp, colour, second_place(colour, k)].astype(F32)
                + r2[k - 1, comp, colour].astype(F32))

    def second_step(k, comp):
        for colour in range(4):
            r2[k - 1, comp, colour] = second_value(k, comp, colour).astype(BF16)
        for colour in range(4):
            second_hop(k, comp, colour).start()

    ring(0, -1, 1, True).wait_recv()
    left_swap(0, 1).start()
    grad_chunk(1)
    ring(0, 1, 1, True).wait_recv()
    left_swap(0, 2).start()
    grad_chunk(2)
    ring(0, 1, 2, True).wait_recv()
    ring(0, -1, 2, True).wait_recv()
    left_swap(0, 3).start()
    grad_chunk(3)

    @pl.loop(0, heads)
    def _(h):
        normed, inverse = normalised(h)
        u = gg[h] * gain_ref[pl.ds(h, 1), :]
        m = jnp.mean(u * normed, axis=-1, keepdims=True)
        p = ((u - normed * m) * inverse).astype(BF16)
        pre[h] = p
        blocks[1, h] = dot_tn(head(qs, h), p).astype(BF16)

    scan_rows(1)

    def mixing_heads(begin, end):
        @pl.loop(begin, end)
        def _(h):
            q, k, v, p = head(qs, h), head(ks, h), head(vs, h), pre[h]
            state = states[0, h]
            left = jnp.where(lower_left, dot_nt(p, v[:half]), 0.0).astype(BF16)
            right = jnp.where(lower_right, dot_nt(p[half:], v[half:]), 0.0).astype(BF16)
            low = dot_nn(left, k[:half]) + dot_nt(p, state)
            cut = pl.ds(pl.multiple_of(h * HEAD_DIM, HEAD_DIM), HEAD_DIM)
            rown[1, :half, cut] = low[:half].astype(BF16)
            rown[1, half:, cut] = (low[half:] + dot_nn(right, k[half:])).astype(BF16)
            att[h, :half] = dot_tn(left, q)
            att[h, half:] = dot_tn(right, q[half:])
            a, b = score_slots(h)
            gg[h, :half] = dot_tn(s1[a, b], p)
            gg[h, half:] = dot_tn(s1[a, b + 1, :half], p[half:])

    mixing_heads(0, heads // 2)
    scan_totals(1)
    mixing_heads(heads // 2, heads)
    right_swap(1).start()
    gather_pass(1)
    scan_results(1)
    for n in range(RING):
        left_swap(0, n).wait_recv()
    right_swap(0).wait_recv()
    zero_step(0, 0)
    zero_step(0, 1)
    scan_end(1)

    @pl.loop(0, heads)
    def _(h):
        k, v = head(ks, h), head(vs, h)
        put_head(2, h, att[h] + dot_nt(v, states[1, h]))
        put_head(3, h, gg[h] + dot_nn(k, states[1, h]))

    right_swap(2).start()
    right_swap(3).start()
    first_step(1, 0)
    ring(1, -1, 1, True).wait_recv()
    left_swap(1, 1).start()
    ring(1, 1, 1, True).wait_recv()
    left_swap(1, 2).start()
    for n in range(3):
        left_swap(1, n).wait_recv()

    @pl.loop(1, 4)
    def _(comp):
        right_swap(comp).wait_recv()
        zero_step(comp, 0)

    first_step(2, 0)
    ring(1, 1, 2, True).wait_recv()
    ring(1, -1, 2, True).wait_recv()
    left_swap(1, 3).start()
    first_step(3, 0)
    left_swap(1, 3).wait_recv()

    @pl.loop(1, 4)
    def _(comp):
        zero_step(comp, 1)

    for k in range(1, RING):
        @pl.loop(1, 4)
        def _(comp, k=k):
            first_step(k, comp)

        if k < RING - 1:
            second_step(k, 0)

    for colour in range(4):
        cut = slice(colour * cols, (colour + 1) * cols)
        out_ref[cut, :] = second_value(RING - 1, 0, colour).T

    for k in range(1, RING - 1):
        @pl.loop(1, 4)
        def _(comp, k=k):
            second_step(k, comp)

    @pl.loop(1, 4)
    def _(comp):
        for colour in range(4):
            cut = slice(colour * cols, (colour + 1) * cols)
            proj_ref[comp - 1, :, cut] = second_value(RING - 1, comp, colour)

    for side in range(2):
        for sign in (1, -1):
            for message in range(3):
                ring(side, sign, message).wait_send()
        for n in range(RING):
            left_swap(side, n).wait_send()
        for o in range(1, ROW):
            row_copy(side, o).wait_send()
            result_copy(side, o).wait_send()
        for o in range(1, RING):
            total_copy(side, o).wait_send()

    @pl.loop(0, 4)
    def _(comp):
        right_swap(comp).wait_send()
        for colour in range(4):
            for k in range(RING - 1):
                first_hop(k, comp, colour).wait_send()
                second_hop(k, comp, colour).wait_send()
            if COLOURS[colour][0]:
                first_hop(0, comp, colour, 1).wait_send()


def body(layer_input, query_rows, key_rows, value_rows, out_weight, norm_gain, cotangent):
    tokens, width = query_rows.shape
    heads = width // HEAD_DIM
    cols = width // 4
    dma = pltpu.SemaphoreType.DMA
    square = (HEAD_DIM, HEAD_DIM)
    anywhere = pl.BlockSpec(memory_space=pl.ANY)
    inside = pl.BlockSpec(memory_space=pltpu.VMEM)
    projection_gradient, output_gradient = pl.pallas_call(
        step_kernel,
        out_shape=(
            jax.ShapeDtypeStruct((3, HEAD_DIM, width), F32),
            jax.ShapeDtypeStruct((width, HEAD_DIM), F32),
        ),
        in_specs=[anywhere] * 5 + [inside, anywhere],
        out_specs=(inside, inside),
        scratch_shapes=[
            pltpu.VMEM((2, RING, RING, 2, HEAD_DIM, tokens), BF16),
            pltpu.VMEM((2, RING, RING, HEAD_DIM, tokens), BF16),
            pltpu.VMEM((4, tokens, width), BF16),
            pltpu.VMEM((4, tokens, width), BF16),
            pltpu.VMEM((tokens, width), BF16),
            pltpu.VMEM((tokens, width), BF16),
            pltpu.VMEM((tokens, width), BF16),
            pltpu.VMEM((2, width, width), BF16),
            pltpu.VMEM((heads, tokens, HEAD_DIM), F32),
            pltpu.VMEM((heads, tokens, HEAD_DIM), F32),
            pltpu.VMEM((heads, tokens, HEAD_DIM), BF16),
            pltpu.VMEM((5, 4, RING * HEAD_DIM, cols), BF16),
            pltpu.VMEM((RING - 1, 4, 4, RING * HEAD_DIM, cols), BF16),
            pltpu.VMEM((4, 4, RING, HEAD_DIM, cols), BF16),
            pltpu.VMEM((RING - 1, 4, 4, HEAD_DIM, cols), BF16),
            pltpu.VMEM((2, ROW) + square, BF16),
            pltpu.VMEM((2, ROW) + square, BF16),
            pltpu.VMEM((2, RING) + square, F32),
            pltpu.VMEM((2, ROW) + square, BF16),
            pltpu.VMEM((2, ROW) + square, BF16),
            dma((9,)),
            dma((2, 2, 3)), dma((2, 2, 3)),
            dma((2, ROW - 1)), dma((2, ROW - 1)),
            dma((2, RING - 1)), dma((2, RING - 1)),
            dma((2, ROW - 1)), dma((2, ROW - 1)),
            dma((2, RING)), dma((2, RING)),
            dma((4,)), dma((4,)),
            dma((RING, 4, 4)), dma((RING, 4, 4)),
            dma((RING - 1, 4, 4)), dma((RING - 1, 4, 4)),
        ],
        compiler_params=pltpu.CompilerParams(
            collective_id=0, has_side_effects=True, vmem_limit_bytes=67043328
        ),
        name="linear_attention_backward",
    )(
        layer_input, query_rows, key_rows, value_rows, out_weight,
        norm_gain.reshape(heads, HEAD_DIM), cotangent,
    )
    return (projection_gradient.transpose(1, 0, 2), output_gradient)


def solution(mesh):
    placed = (
        P("seq", "head"),
        P("seq", "head"),
        P("seq", "head"),
        P("seq", "head"),
        P("head", None),
        P("head"),
        P("seq", "head"),
    )
    return jax.shard_map(
        body,
        mesh=mesh,
        in_specs=placed,
        out_specs=(P("seq", None, "head"), P("head", "seq")),
        check_vma=False,
    )
```

```python
import jax
import jax.numpy as jnp
from jax import lax
from jax.experimental import pallas as pl
from jax.experimental.pallas import tpu as pltpu
from jax.sharding import PartitionSpec as P

HEAD_DIM = 128
F32 = jnp.float32
BF16 = jnp.bfloat16
MESH_ID = pl.DeviceIdType.MESH
COLOURS = ((True, 1), (True, -1), (False, 1), (False, -1))
RING = 4
ROW = 8


def dot_nn(a, b):
    return jnp.dot(a, b, preferred_element_type=F32)


def dot_nt(a, b):
    return lax.dot_general(a, b, (((1,), (1,)), ((), ())), preferred_element_type=F32)


def dot_tn(a, b):
    return jnp.dot(a.T, b, preferred_element_type=F32)


def step_kernel(
    x_hbm, q_hbm, k_hbm, v_hbm, w_hbm, gain_ref, cot_hbm,
    proj_ref, out_ref,
    lown, lpar, rown, rpar, qs, ks, vs, wbuf, att, gg, pre, s1, r1, acc, r2,
    blocks, gathered, totals, results, states,
    load_sem, g_send, g_recv, row_send, row_recv, tot_send, tot_recv, res_send, res_recv,
    lp_send, lp_recv, rp_send, rp_recv, s1_send, s1_recv, s2_send, s2_recv,
):
    me = lax.axis_index("seq")
    y = lax.axis_index("head")
    core = lax.rem(me, 2)
    z = lax.rem(lax.div(me, 2), RING)
    x = lax.div(me, ROW)
    j = lax.rem(me, ROW)
    tokens = qs.shape[0]
    width = qs.shape[1]
    half = tokens // 2
    heads = width // HEAD_DIM
    cols = s1.shape[-1]
    rows = RING * HEAD_DIM

    def at(x_, z_, core_):
        return {"seq": x_ * ROW + z_ * 2 + core_}

    def row_peer(j_):
        return {"seq": x * ROW + j_}

    def turn(a, n=RING):
        return lax.rem(a + 2 * n, n)

    def step_of(is_z, sign):
        return at(x, turn(z + sign), core) if is_z else at(turn(x + sign), z, core)

    partner = at(x, z, 1 - core)

    def remote(source, target, send, recv, who):
        return pltpu.make_async_remote_copy(
            source, target, send, recv, device_id=who, device_id_type=MESH_ID)

    def weight_load(n, chunk):
        start = pl.multiple_of(chunk * width, width)
        return pltpu.make_async_copy(
            w_hbm.at[:, pl.ds(start, width)], wbuf.at[n % 2], load_sem.at[5 + n])

    order = (y, turn(y - 1), turn(y + 1), turn(y + 2))
    load_cot = pltpu.make_async_copy(cot_hbm, rown.at[1], load_sem.at[0])
    load_k = pltpu.make_async_copy(k_hbm, ks, load_sem.at[1])
    load_v = pltpu.make_async_copy(v_hbm, vs, load_sem.at[2])
    load_x = pltpu.make_async_copy(x_hbm, rown.at[2], load_sem.at[3])
    load_q = pltpu.make_async_copy(q_hbm, qs, load_sem.at[4])
    for load in (load_cot, load_k, load_v):
        load.start()

    barrier = pltpu.get_barrier_semaphore()
    peers = [row_peer(turn(j + o, ROW)) for o in range(1, ROW)]
    peers += [at(turn(x + o), z, core) for o in range(1, RING)]
    peers += [{"head": turn(y + 1)}, {"head": turn(y - 1)}]
    for who in peers:
        pl.semaphore_signal(barrier, inc=1, device_id=who, device_id_type=MESH_ID)

    def transpose_in(side, stage):
        for i in range(heads):
            lown[side, y, i // 2, i % 2] = rown[stage, :, i * HEAD_DIM:(i + 1) * HEAD_DIM].T

    load_cot.wait()
    load_x.start()
    load_q.start()
    weight_load(0, order[0]).start()
    weight_load(1, order[1]).start()
    transpose_in(0, 1)
    pl.semaphore_wait(barrier, len(peers))

    def ring(side, sign, message, receiving=False):
        first = 0 if sign > 0 else 2
        part = first if message != 1 else 2 - first
        source = y if message < 2 else turn(y - sign)
        if receiving:
            source = turn(source - sign)
        place = lown.at[side, source, pl.ds(part, 2)]
        n = 0 if sign > 0 else 1
        return remote(
            place, place, g_send.at[side, n, message], g_recv.at[side, n, message],
            {"head": turn(y + sign)})

    def gather_own(side):
        for message in (0, 1):
            for sign in (1, -1):
                ring(side, sign, message).start()

    def gather_pass(side):
        for sign in (1, -1):
            ring(side, sign, 0, True).wait_recv()
            ring(side, sign, 2).start()

    gather_own(0)

    def row_copy(n, o, receiving=False):
        if receiving:
            place = turn(j - o, ROW)
            return remote(blocks.at[n, place], gathered.at[n, place],
                          row_send.at[n, o - 1], row_recv.at[n, o - 1], row_peer(place))
        to = turn(j + o, ROW)
        return remote(blocks.at[n, to], gathered.at[n, j],
                      row_send.at[n, o - 1], row_recv.at[n, o - 1], row_peer(to))

    def total_copy(n, o, receiving=False):
        place = turn(x - o) if receiving else x
        return remote(totals.at[n, place], totals.at[n, place],
                      tot_send.at[n, o - 1], tot_recv.at[n, o - 1], at(turn(x + o), z, core))

    def result_copy(n, o, receiving=False):
        if receiving:
            place = turn(j - o, ROW)
            return remote(results.at[n, place], states.at[n, place],
                          res_send.at[n, o - 1], res_recv.at[n, o - 1], row_peer(place))
        to = turn(j + o, ROW)
        return remote(results.at[n, to], states.at[n, j],
                      res_send.at[n, o - 1], res_recv.at[n, o - 1], row_peer(to))

    def scan_rows(n):
        gathered[n, j] = blocks[n, j]
        for o in range(1, ROW):
            row_copy(n, o).start()

    def scan_totals(n):
        for o in range(1, ROW):
            row_copy(n, o, True).wait_recv()
        total = gathered[n, 0].astype(F32)
        for i in range(1, ROW):
            total = total + gathered[n, i].astype(F32)
        totals[n, x] = total
        for o in range(1, RING):
            total_copy(n, o).start()

    def scan_results(n):
        for o in range(1, RING):
            total_copy(n, o, True).wait_recv()
        running = jnp.zeros((HEAD_DIM, HEAD_DIM), F32)
        for i in range(RING):
            counts = (i > x) if n else (i < x)
            running = running + jnp.where(counts, totals[n, i], 0.0)
        for i in (reversed(range(ROW)) if n else range(ROW)):
            results[n, i] = running.astype(BF16)
            running = running + gathered[n, i].astype(F32)
        states[n, j] = results[n, j]
        for o in range(1, ROW):
            result_copy(n, o).start()

    def scan_end(n):
        for o in range(1, ROW):
            result_copy(n, o, True).wait_recv()

    def head(ref, h):
        return ref[:, pl.ds(pl.multiple_of(h * HEAD_DIM, HEAD_DIM), HEAD_DIM)]

    def put_head(comp, h, value):
        rown[comp, :, pl.ds(pl.multiple_of(h * HEAD_DIM, HEAD_DIM), HEAD_DIM)] = value.astype(BF16)

    load_k.wait()
    load_v.wait()

    @pl.loop(0, heads)
    def _(h):
        blocks[0, h] = dot_tn(head(ks, h), head(vs, h)).astype(BF16)

    scan_rows(0)
    load_x.wait()
    transpose_in(1, 2)
    load_q.wait()
    scan_totals(0)

    lower_left = (
        lax.broadcasted_iota(jnp.int32, (tokens, half), 0)
        >= lax.broadcasted_iota(jnp.int32, (tokens, half), 1)
    )
    lower_right = lower_left[:half]

    def score_slots(h):
        return lax.div(h, 2), lax.rem(h, 2) * 2

    @pl.loop(0, heads)
    def _(h):
        q, k, v = head(qs, h), head(ks, h), head(vs, h)
        left = jnp.where(lower_left, dot_nt(q, k[:half]), 0.0).astype(BF16)
        right = jnp.where(lower_right, dot_nt(q[half:], k[half:]), 0.0).astype(BF16)
        a, b = score_slots(h)
        s1[a, b] = left
        s1[a, b + 1, :half] = right
        att[h, :half] = dot_nn(left[:half], v[:half])
        att[h, half:] = dot_nn(left[half:], v[:half]) + dot_nn(right, v[half:])

    scan_results(0)

    def grad_chunk(n):
        weight_load(n, order[n]).wait()

        @pl.loop(0, RING)
        def _(t):
            w = wbuf[n % 2, pl.ds(pl.multiple_of(t * 2 * HEAD_DIM, 2 * HEAD_DIM), 2 * HEAD_DIM), :]
            value = dot_nn(w, lown[0, order[n]].reshape(width, tokens)).T
            for i in range(2):
                piece = value[:, i * HEAD_DIM:(i + 1) * HEAD_DIM]
                if n:
                    piece = piece + gg[2 * t + i]
                gg[2 * t + i] = piece

        if n + 2 < RING:
            weight_load(n + 2, order[n + 2]).start()

    gather_pass(0)
    gather_own(1)
    grad_chunk(0)

    def normalised(h):
        a = att[h]
        inverse = lax.rsqrt(jnp.mean(a * a, axis=-1, keepdims=True) + 1e-05)
        return a * inverse, inverse

    scan_end(0)

    @pl.loop(0, heads)
    def _(h):
        att[h] = att[h] + dot_nn(head(qs, h), states[0, h])
        normed, _ = normalised(h)
        put_head(0, h, normed * gain_ref[pl.ds(h, 1), :])

    def left_swap(side, piece):
        return remote(lown.at[side, piece, :, 1 - core], lpar.at[side, piece],
                      lp_send.at[side, piece], lp_recv.at[side, piece], partner)

    def right_swap(comp):
        return remote(rown.at[comp], rpar.at[comp], rp_send.at[comp], rp_recv.at[comp], partner)

    right_swap(0).start()
    ring(0, 1, 1, True).wait_recv()
    left_swap(0, order[0]).start()
    left_swap(0, order[1]).start()
    grad_chunk(1)
    ring(0, -1, 1, True).wait_recv()
    left_swap(0, order[2]).start()
    grad_chunk(2)
    ring(0, 1, 2, True).wait_recv()
    ring(0, -1, 2, True).wait_recv()
    left_swap(0, order[3]).start()
    grad_chunk(3)

    @pl.loop(0, heads)
    def _(h):
        normed, inverse = normalised(h)
        u = gg[h] * gain_ref[pl.ds(h, 1), :]
        m = jnp.mean(u * normed, axis=-1, keepdims=True)
        p = ((u - normed * m) * inverse).astype(BF16)
        pre[h] = p
        blocks[1, h] = dot_tn(head(qs, h), p).astype(BF16)

    scan_rows(1)

    def term(comp, colour, d):
        side = lax.div(comp + 3, 4)
        cut = slice(colour * cols, (colour + 1) * cols)
        if COLOURS[colour][0]:
            mine, other = lown[side, :, d, core], lpar[side, :, d]
        else:
            mine, other = lown[side, d, :, core], lpar[side, d]
        value = dot_nn(mine.reshape(rows, tokens), rown[comp, :, cut])
        return value + dot_nn(other.reshape(rows, tokens), rpar[comp, :, cut])

    def first_hop(k, comp, colour):
        source = s1.at[comp, colour] if k == 0 else r1.at[k - 1, comp, colour]
        return remote(source, r1.at[k, comp, colour], s1_send.at[k, comp, colour],
                      s1_recv.at[k, comp, colour], step_of(*COLOURS[colour]))

    def second_hop(k, comp, colour):
        is_z, sign = COLOURS[colour]
        place = x if is_z else z
        source = acc.at[comp, colour, turn(place - sign)] if k == 0 else r2.at[k - 1, comp, colour]
        return remote(source, r2.at[k, comp, colour], s2_send.at[k, comp, colour],
                      s2_recv.at[k, comp, colour], step_of(not is_z, sign))

    def first_step(k, comp):
        for colour, (is_z, sign) in enumerate(COLOURS):
            value = term(comp, colour, turn((z if is_z else x) - sign * (1 + k)))
            if k:
                first_hop(k - 1, comp, colour).wait_recv()
                value = value + r1[k - 1, comp, colour].astype(F32)
            value = value.astype(BF16)
            if k == 0:
                s1[comp, colour] = value
            elif k < RING - 1:
                r1[k - 1, comp, colour] = value
            else:
                acc[comp, colour] = value.reshape(RING, HEAD_DIM, cols)
        for colour in range(4):
            if k < RING - 1:
                first_hop(k, comp, colour).start()
            else:
                second_hop(0, comp, colour).start()

    def second_value(k, comp, colour):
        is_z, sign = COLOURS[colour]
        e = turn((x if is_z else z) - sign * (1 + k))
        second_hop(k - 1, comp, colour).wait_recv()
        return acc[comp, colour, e].astype(F32) + r2[k - 1, comp, colour].astype(F32)

    def second_step(k, comp):
        for colour in range(4):
            r2[k - 1, comp, colour] = second_value(k, comp, colour).astype(BF16)
        for colour in range(4):
            second_hop(k, comp, colour).start()

    scan_totals(1)

    @pl.loop(0, heads)
    def _(h):
        q, k, v, p = head(qs, h), head(ks, h), head(vs, h), pre[h]
        state = states[0, h]
        left = jnp.where(lower_left, dot_nt(p, v[:half]), 0.0).astype(BF16)
        right = jnp.where(lower_right, dot_nt(p[half:], v[half:]), 0.0).astype(BF16)
        old = dot_nt(p, state)
        low = dot_nn(left, k[:half]) + old
        cut = pl.ds(pl.multiple_of(h * HEAD_DIM, HEAD_DIM), HEAD_DIM)
        rown[1, :half, cut] = low[:half].astype(BF16)
        rown[1, half:, cut] = (low[half:] + dot_nn(right, k[half:])).astype(BF16)
        att[h, :half] = dot_tn(left, q)
        att[h, half:] = dot_tn(right, q[half:])
        a, b = score_slots(h)
        gg[h, :half] = dot_tn(s1[a, b], p)
        gg[h, half:] = dot_tn(s1[a, b + 1, :half], p[half:])

    scan_results(1)
    right_swap(1).start()
    gather_pass(1)
    for piece in order:
        left_swap(0, piece).wait_recv()
    right_swap(0).wait_recv()
    first_step(0, 0)
    scan_end(1)

    @pl.loop(0, heads)
    def _(h):
        k, v = head(ks, h), head(vs, h)
        put_head(2, h, att[h] + dot_nt(v, states[1, h]))
        put_head(3, h, gg[h] + dot_nn(k, states[1, h]))

    right_swap(2).start()
    right_swap(3).start()
    first_step(1, 0)
    left_swap(1, order[0]).start()
    ring(1, 1, 1, True).wait_recv()
    left_swap(1, order[1]).start()
    ring(1, -1, 1, True).wait_recv()
    left_swap(1, order[2]).start()
    first_step(2, 0)
    ring(1, 1, 2, True).wait_recv()
    ring(1, -1, 2, True).wait_recv()
    left_swap(1, order[3]).start()
    first_step(3, 0)
    for comp in range(1, 4):
        right_swap(comp).wait_recv()
    for piece in order:
        left_swap(1, piece).wait_recv()

    for k in range(RING):
        @pl.loop(1, 4)
        def _(comp, k=k):
            first_step(k, comp)

        if 0 < k < RING - 1:
            second_step(k, 0)

    for colour in range(4):
        cut = slice(colour * cols, (colour + 1) * cols)
        out_ref[cut, :] = second_value(RING - 1, 0, colour).T

    for k in range(1, RING - 1):
        @pl.loop(1, 4)
        def _(comp, k=k):
            second_step(k, comp)

    @pl.loop(1, 4)
    def _(comp):
        for colour in range(4):
            cut = slice(colour * cols, (colour + 1) * cols)
            proj_ref[comp - 1, :, cut] = second_value(RING - 1, comp, colour)

    for side in range(2):
        for sign in (1, -1):
            for message in range(3):
                ring(side, sign, message).wait_send()
        for piece in order:
            left_swap(side, piece).wait_send()
        for o in range(1, ROW):
            row_copy(side, o).wait_send()
            result_copy(side, o).wait_send()
        for o in range(1, RING):
            total_copy(side, o).wait_send()

    @pl.loop(0, 4)
    def _(comp):
        right_swap(comp).wait_send()
        for colour in range(4):
            for k in range(RING - 1):
                first_hop(k, comp, colour).wait_send()
                second_hop(k, comp, colour).wait_send()


def body(layer_input, query_rows, key_rows, value_rows, out_weight, norm_gain, cotangent):
    tokens, width = query_rows.shape
    heads = width // HEAD_DIM
    cols = width // 4
    dma = pltpu.SemaphoreType.DMA
    square = (HEAD_DIM, HEAD_DIM)
    anywhere = pl.BlockSpec(memory_space=pl.ANY)
    inside = pl.BlockSpec(memory_space=pltpu.VMEM)
    projection_gradient, output_gradient = pl.pallas_call(
        step_kernel,
        out_shape=(
            jax.ShapeDtypeStruct((3, HEAD_DIM, width), F32),
            jax.ShapeDtypeStruct((width, HEAD_DIM), F32),
        ),
        in_specs=[anywhere] * 5 + [inside, anywhere],
        out_specs=(inside, inside),
        scratch_shapes=[
            pltpu.VMEM((2, RING, RING, 2, HEAD_DIM, tokens), BF16),
            pltpu.VMEM((2, RING, RING, HEAD_DIM, tokens), BF16),
            pltpu.VMEM((4, tokens, width), BF16),
            pltpu.VMEM((4, tokens, width), BF16),
            pltpu.VMEM((tokens, width), BF16),
            pltpu.VMEM((tokens, width), BF16),
            pltpu.VMEM((tokens, width), BF16),
            pltpu.VMEM((2, width, width), BF16),
            pltpu.VMEM((heads, tokens, HEAD_DIM), F32),
            pltpu.VMEM((heads, tokens, HEAD_DIM), F32),
            pltpu.VMEM((heads, tokens, HEAD_DIM), BF16),
            pltpu.VMEM((4, 4, RING * HEAD_DIM, cols), BF16),
            pltpu.VMEM((RING - 1, 4, 4, RING * HEAD_DIM, cols), BF16),
            pltpu.VMEM((4, 4, RING, HEAD_DIM, cols), BF16),
            pltpu.VMEM((RING - 1, 4, 4, HEAD_DIM, cols), BF16),
            pltpu.VMEM((2, ROW) + square, BF16),
            pltpu.VMEM((2, ROW) + square, BF16),
            pltpu.VMEM((2, RING) + square, F32),
            pltpu.VMEM((2, ROW) + square, BF16),
            pltpu.VMEM((2, ROW) + square, BF16),
            dma((9,)),
            dma((2, 2, 3)), dma((2, 2, 3)),
            dma((2, ROW - 1)), dma((2, ROW - 1)),
            dma((2, RING - 1)), dma((2, RING - 1)),
            dma((2, ROW - 1)), dma((2, ROW - 1)),
            dma((2, RING)), dma((2, RING)),
            dma((4,)), dma((4,)),
            dma((RING - 1, 4, 4)), dma((RING - 1, 4, 4)),
            dma((RING - 1, 4, 4)), dma((RING - 1, 4, 4)),
        ],
        compiler_params=pltpu.CompilerParams(
            collective_id=0, has_side_effects=True, vmem_limit_bytes=67043328
        ),
        name="linear_attention_backward",
    )(
        layer_input, query_rows, key_rows, value_rows, out_weight,
        norm_gain.reshape(heads, HEAD_DIM), cotangent,
    )
    return (projection_gradient.transpose(1, 0, 2), output_gradient)


def solution(mesh):
    placed = (
        P("seq", "head"),
        P("seq", "head"),
        P("seq", "head"),
        P("seq", "head"),
        P("head", None),
        P("head"),
        P("seq", "head"),
    )
    return jax.shard_map(
        body,
        mesh=mesh,
        in_specs=placed,
        out_specs=(P("seq", None, "head"), P("head", "seq")),
        check_vma=False,
    )
```
